128 devices in a mesh: seq: 16 (over x, z), head: 8 (over y, core).
Axes of the slice: x: 4, y: 4, z: 4, core: 2. Of those that a mesh axis runs over, the one named last changes fastest.
Arguments:
- prompt_keys: bfloat16 [16384, 2048], P('seq', 'head'), may hold values from -6 to 6
- prompt_values: bfloat16 [16384, 4096], P('seq', 'head'), may hold values from -6 to 6
- prompt_input: float32 [8, 16384], P('head', 'seq'), may hold values from -3 to 0
- prompt_forget: float32 [8, 16384], P('head', 'seq'), may hold values from 0.4 to 17
- prompt_lengths: int32 [4], replicated, may hold values from 1 to 8192, 16384 in all
- response_prompt: int32 [32, 1], replicated, may hold values from 0 to 3
- resp_queries: bfloat16 [32, 512, 2048], P('seq', None, 'head'), may hold values from -6 to 6
- resp_keys: bfloat16 [32, 512, 2048], P('seq', None, 'head'), may hold values from -6 to 6
- resp_values: bfloat16 [32, 512, 4096], P('seq', None, 'head'), may hold values from -6 to 6
- resp_input: float32 [8, 32, 512], P('head', 'seq'), may hold values from -3 to 0
- resp_forget: float32 [8, 32, 512], P('head', 'seq'), may hold values from 0.4 to 17
- norm_gain: float32 [4096], P('head'), may hold values from 0.1 to 1.9
- out_grad: bfloat16 [32, 512, 4096], P('seq', None, 'head'), may hold values from -6 to 6
Outputs:
- resp_out: bfloat16 [32, 512, 4096], P('seq', None, 'head')
- prompt_key_grad: bfloat16 [16384, 2048], P('seq', 'head')
- prompt_value_grad: bfloat16 [16384, 4096], P('seq', 'head')
The draws below stay inside these ranges and needn't reach their ends.
Inputs may be any that keep to these rules, and one draw needn't show every extreme that they name: `prompt_lengths`: prompt p covers the window positions from the sum of the earlier lengths onward; the lengths sum to 16384 and the longest is exactly half of 16384. `response_prompt`: every prompt is continued by at least one response.
All inputs are finite; a program needn't handle non-finite values.
Results may differ from the reference program's by a relative error of at most 0.025.
Values may be sent and summed in bfloat16 or wider, within the bound.
No kernel may reach another device: no remote copies, remote signals or barrier semaphores. Data moves between devices by JAX's collectives and lax.ppermute only.
A program may use at most 64 MiB of HBM per device.

```python
import math
import jax
import jax.numpy as jnp
import numpy as np
from jax import lax

MLSTM_HEADS = 8
DK = 256
DV = 512
PROMPTS = 4
WIN_DEV = 1024
WINDOW_TOTAL = 16384
RESP = 32
RLEN = 512


def forget_field(key, groups, rows, chain, slow_count):
    keys_all = jax.random.split(key, 5)
    shuffled = jax.random.permutation(keys_all[0], MLSTM_HEADS)
    is_slow = shuffled < slow_count
    slow_rate = jnp.exp(jax.random.uniform(keys_all[1], (MLSTM_HEADS,), minval=jnp.log(0.03), maxval=jnp.log(0.3))) / chain
    fast_rate = jnp.exp(-jax.random.uniform(keys_all[2], (MLSTM_HEADS,), minval=jnp.log(20.0), maxval=jnp.log(60.0)))
    base_rate = jnp.where(is_slow, slow_rate, fast_rate)
    jitter = jnp.exp(jax.random.uniform(keys_all[3], (MLSTM_HEADS, groups, rows), minval=-0.69, maxval=0.69))
    block_factor = jnp.exp(jax.random.uniform(keys_all[4], (MLSTM_HEADS, groups, 1), minval=-0.69, maxval=0.69))
    step_rate = base_rate[:, None, None] * jitter * block_factor
    return -jnp.log(jnp.expm1(step_rate))


def add_spikes(key, gate_preactivation):
    key_location, key_keep = jax.random.split(key)
    spike_position = jax.random.randint(key_location, gate_preactivation.shape[:2] + (2,), 0, gate_preactivation.shape[2])
    target_positions = jnp.arange(gate_preactivation.shape[2])
    is_spike = jnp.any(target_positions[None, None, :, None] == spike_position[:, :, None, :], axis=-1)
    kept_entries = jax.random.uniform(key_keep, gate_preactivation.shape, minval=0.6, maxval=0.8)
    return jnp.where(is_spike, jnp.log(kept_entries / (1.0 - kept_entries)), gate_preactivation)


def draw_prompt_forget(key, part):
    slow_count = MLSTM_HEADS // 2
    blocks = WINDOW_TOTAL // WIN_DEV
    gate_preactivation = forget_field(key, blocks, WIN_DEV, WINDOW_TOTAL, slow_count).reshape(MLSTM_HEADS, 1, WINDOW_TOTAL)
    return add_spikes(jax.random.fold_in(key, 7), gate_preactivation).reshape(MLSTM_HEADS, WINDOW_TOTAL)


def draw_resp_forget(key, part):
    slow_count = MLSTM_HEADS // 2
    gate_preactivation = forget_field(key, RESP, RLEN, RLEN, slow_count)
    return add_spikes(jax.random.fold_in(key, 7), gate_preactivation)


def block_levels(rng, dims, cuts, smallest, largest):
    factor_of = 1.0
    for axis_at, parts in cuts:
        draws = jax.random.uniform(jax.random.fold_in(jax.random.fold_in(rng, 6), axis_at), (parts,), jnp.float32, smallest / len(cuts), largest / len(cuts))
        factor_of = factor_of * jnp.repeat(jnp.exp(draws), dims[axis_at] // parts).reshape((-1,) + (1,) * (len(dims) - 1 - axis_at))
    return factor_of


def different_ones(own_key, rows, amount, top, lift):
    order = jax.random.permutation(jax.random.fold_in(own_key, 1), amount)
    boost = order
    for power in range(3):
        boost = boost * boost // amount
    boost = boost * lift // amount
    chance = jax.random.randint(jax.random.fold_in(own_key, 2), (rows, amount), 0, 4096) + boost
    fixed_rows = jax.random.permutation(jax.random.fold_in(own_key, 3), rows)[jnp.arange(amount) % rows]
    chance = jnp.where(jnp.arange(rows)[:, None] == fixed_rows[None, :], 1 << 14, chance)
    priority = chance * amount + jnp.arange(amount)
    return lax.top_k(priority.astype(jnp.int32), top)[1].astype(jnp.int32)


def length_profile(count, total, reach, lean):
    portions = [(1 << 20) // math.isqrt(grade ** lean) + 1 for grade in range(2, count + 1)]
    spare, holding = total - reach - (count - 1), [1] * (count - 1)
    while spare > 0:
        candidates = [i for i in range(count - 1) if holding[i] < reach]
        whole, remaining = sum([portions[i] for i in candidates]), spare
        for i in candidates:
            extra = min(reach - holding[i], max(1, remaining * portions[i] // whole), spare)
            holding[i] = holding[i] + extra
            spare = spare - extra
    return np.array([reach] + holding)


def ragged(rng, amount, total, limit, skew):
    if amount == 2:
        one = jax.random.randint(rng, (), max(1, total - limit), min(limit, total - 1) + 1)
        return jnp.stack([one, total - one])
    sizes = jnp.asarray(length_profile(amount, total, limit, skew), jnp.int32)
    twos = (amount - 1) // 2
    giver, receiver = sizes[1:1 + 2 * twos:2], sizes[2:2 + 2 * twos:2]
    room = jnp.minimum(giver - 1, limit - receiver)
    moved = jax.random.randint(jax.random.fold_in(rng, 1), (twos,), 0, 1 << 20) % (room + 1)
    sizes = sizes.at[1:1 + 2 * twos:2].set(giver - moved).at[2:2 + 2 * twos:2].set(receiver + moved)
    return sizes[jax.random.permutation(jax.random.fold_in(rng, 2), amount)]


def gaussian(own_key, shape, scale, reach, cuts=(), kind=jnp.bfloat16):
    entries = jax.random.normal(own_key, shape, jnp.float32) * scale
    if len(cuts) > 0:
        entries = block_levels(own_key, shape, cuts, -0.22, 0.18) * entries
    return jnp.clip(entries, min=-reach, max=reach).astype(kind)


def setup_inputs(seed: int = 0) -> dict:
    streams_of = jax.random.split(jax.random.key(seed), 14)
    return {
        "prompt_keys": gaussian(streams_of[0], (WINDOW_TOTAL, MLSTM_HEADS * DK), 1.0, 6.0, ((0, 16), (1, 8))),
        "prompt_values": gaussian(streams_of[1], (WINDOW_TOTAL, MLSTM_HEADS * DV), 1.0, 6.0, ((0, 16), (1, 8))),
        "prompt_input": jnp.clip(-3.0 + 3.0 * jax.random.uniform(streams_of[2], (MLSTM_HEADS, WINDOW_TOTAL), jnp.float32) ** block_levels(streams_of[2], (MLSTM_HEADS, WINDOW_TOTAL), ((0, 8), (1, 16)), -0.2, 0.2), -3.0, 0.0),
        "prompt_forget": draw_prompt_forget(jax.random.fold_in(streams_of[13], 71), 0),
        "prompt_lengths": ragged(streams_of[4], PROMPTS, WINDOW_TOTAL, WINDOW_TOTAL // 2, 2).astype(jnp.int32),
        "response_prompt": different_ones(streams_of[5], RESP, PROMPTS, 1, 2048),
        "resp_queries": gaussian(streams_of[6], (RESP, RLEN, MLSTM_HEADS * DK), 1.0, 6.0, ((0, 16), (2, 8))),
        "resp_keys": gaussian(streams_of[7], (RESP, RLEN, MLSTM_HEADS * DK), 1.0, 6.0, ((0, 16), (2, 8))),
        "resp_values": gaussian(streams_of[8], (RESP, RLEN, MLSTM_HEADS * DV), 1.0, 6.0, ((0, 16), (2, 8))),
        "resp_input": jnp.clip(-3.0 + 3.0 * jax.random.uniform(streams_of[9], (MLSTM_HEADS, RESP, RLEN), jnp.float32) ** block_levels(streams_of[9], (MLSTM_HEADS, RESP, RLEN), ((0, 8), (1, 16)), -0.2, 0.2), -3.0, 0.0),
        "resp_forget": draw_resp_forget(jax.random.fold_in(streams_of[13], 71), 0),
        "norm_gain": jnp.clip(1.0 + 0.18 * jax.random.normal(streams_of[11], (MLSTM_HEADS * DV,), jnp.float32), 0.1, 1.9),
        "out_grad": gaussian(streams_of[12], (RESP, RLEN, MLSTM_HEADS * DV), 1.0, 6.0, ((0, 16), (2, 8))),
    }


def respond(queries, key_rows, values, gate_in, gate_forget, state_init, norm_init):
    key_scale = queries.shape[-1] ** (-0.5)
    length = queries.shape[0]
    cumulative = jnp.cumsum(jax.nn.log_sigmoid(gate_forget))
    scores = jnp.dot(queries, key_rows.T, preferred_element_type=jnp.float32) * key_scale
    target_positions = jnp.arange(length)
    causal = target_positions[:, None] >= target_positions[None, :]
    decays = jnp.where(causal, cumulative[:, None] - cumulative[None, :] + gate_in[None, :], -1e+30)
    mixing = (scores * jnp.exp(decays)).astype(jnp.bfloat16)
    lifted = jnp.exp(cumulative) * key_scale
    numerator = jnp.dot(mixing, values, preferred_element_type=jnp.float32) + lifted[:, None] * jnp.dot(queries, state_init, preferred_element_type=jnp.float32)
    denominator = jnp.dot(mixing, jnp.ones((length,), jnp.bfloat16), preferred_element_type=jnp.float32) + lifted * jnp.dot(queries, norm_init, preferred_element_type=jnp.float32)
    return (numerator, denominator, lifted)

def reference(prompt_keys, prompt_values, prompt_input, prompt_forget, prompt_lengths, response_prompt, resp_queries, resp_keys, resp_values, resp_input, resp_forget, norm_gain, out_grad):
    largest_magnitude = lax.Precision.HIGHEST
    positions = jnp.arange(WINDOW_TOTAL, dtype=jnp.int32)
    prompt_ends = jnp.cumsum(prompt_lengths).astype(jnp.int32)
    prompt_id = lax.optimization_barrier(jnp.sum((positions[:, None] >= prompt_ends[None, :]).astype(jnp.int32), axis=1))
    prompt_range = jnp.arange(PROMPTS, dtype=jnp.int32)
    member = prompt_id[:, None] == prompt_range[None, :]
    member_f = member.astype(jnp.float32)
    log_forget = jax.nn.log_sigmoid(prompt_forget)
    masked = log_forget[:, :, None] * member_f[None]
    suffix = jnp.flip(jnp.cumsum(jnp.flip(masked, 1), 1), 1) - masked
    weight = jnp.exp(prompt_input + lax.optimization_barrier(jnp.sum(suffix * member_f[None], axis=2)))
    key_heads = jnp.transpose(prompt_keys.reshape(WINDOW_TOTAL, MLSTM_HEADS, DK), (1, 0, 2))
    value_heads = jnp.transpose(prompt_values.reshape(WINDOW_TOTAL, MLSTM_HEADS, DV), (1, 0, 2))
    weighted = (key_heads.astype(jnp.float32) * weight[:, :, None]).astype(jnp.bfloat16)
    block_rows = min(256, WINDOW_TOTAL)
    block_count = WINDOW_TOTAL // block_rows
    weighted_blocks = jnp.transpose(weighted.reshape(MLSTM_HEADS, block_count, block_rows, DK), (1, 0, 2, 3))
    value_blocks = jnp.transpose(value_heads.reshape(MLSTM_HEADS, block_count, block_rows, DV), (1, 0, 2, 3))
    id_blocks = prompt_id.reshape(block_count, block_rows)
    member_blocks = member.reshape(block_count, block_rows, PROMPTS)

    def state_step(carry, items):
        weight_rows, value_rows, rows_id, rows_member = items
        weight_single_precise = weight_rows.astype(jnp.float32)
        value_single_precise = value_rows.astype(jnp.float32)

        def single(unused):
            part = jnp.einsum('jgf,jgp->jfp', weight_single_precise, value_single_precise, precision=largest_magnitude)
            return jnp.where((prompt_range == rows_id[0])[None, :, None, None], part[:, None], 0.0)

        def several(unused):
            spread = jnp.where(rows_member[None, :, :, None], weight_single_precise[:, :, None, :], 0.0)
            return jnp.einsum('htpk,htv->hpkv', spread, value_single_precise, precision=largest_magnitude)
        return (carry + lax.cond(rows_id[0] == rows_id[-1], single, several, 0), None)
    states_init = jnp.zeros((MLSTM_HEADS, PROMPTS, DK, DV), jnp.float32)
    states, unused_out = lax.scan(state_step, states_init, (weighted_blocks, value_blocks, id_blocks, member_blocks))
    norms = jnp.einsum('tp,htk->hpk', member_f, weighted.astype(jnp.float32), precision=largest_magnitude)
    state_low = states.astype(jnp.bfloat16)
    norm_low = norms.astype(jnp.bfloat16)
    picks = response_prompt[:, 0]
    query_heads = jnp.transpose(resp_queries.reshape(RESP, RLEN, MLSTM_HEADS, DK), (2, 0, 1, 3))
    rkey_heads = jnp.transpose(resp_keys.reshape(RESP, RLEN, MLSTM_HEADS, DK), (2, 0, 1, 3))
    rvalue_heads = jnp.transpose(resp_values.reshape(RESP, RLEN, MLSTM_HEADS, DV), (2, 0, 1, 3))

    def head_forward(items):
        queries, key_rows, values, gate_in, gate_forget, state_head, norm_head = items
        return jax.vmap(respond)(queries, key_rows, values, gate_in, gate_forget, state_head[picks], norm_head[picks])
    numerator, denominator, lifted = lax.map(head_forward, (query_heads, rkey_heads, rvalue_heads, resp_input, resp_forget, state_low, norm_low))
    bound = jnp.sqrt(denominator * denominator + 1.0)
    hidden = numerator / bound[..., None]
    total_squares = lax.optimization_barrier(jnp.sum(hidden * hidden, axis=(0, 3)))
    inv_rms = lax.rsqrt(total_squares / (MLSTM_HEADS * DV) + 1e-06)
    gain = norm_gain.reshape(MLSTM_HEADS, DV)[:, None, None, :]
    scaled = hidden * gain * inv_rms[None, :, :, None]
    resp_out = jnp.transpose(scaled, (1, 2, 0, 3)).reshape(RESP, RLEN, MLSTM_HEADS * DV).astype(jnp.bfloat16)
    grad_heads = jnp.transpose(out_grad.reshape(RESP, RLEN, MLSTM_HEADS, DV), (2, 0, 1, 3)).astype(jnp.float32)
    dots = lax.optimization_barrier(jnp.sum(grad_heads * gain * hidden, axis=(0, 3)))
    d_hidden = gain * grad_heads * inv_rms[None, :, :, None] - hidden * (dots * inv_rms ** 3 / (MLSTM_HEADS * DV))[None, :, :, None]
    d_numer = d_hidden / bound[..., None]
    d_denom = -lax.optimization_barrier(jnp.sum(d_hidden * hidden, axis=-1)) * denominator / (bound * bound)
    lift_numer = (lifted[..., None] * d_numer).astype(jnp.bfloat16)
    lift_denom = (lifted * d_denom).astype(jnp.bfloat16)
    d_state = jnp.einsum('hrlk,hrlv->hrkv', query_heads.astype(jnp.float32), lift_numer.astype(jnp.float32), precision=largest_magnitude)
    d_norm = jnp.einsum('hrlk,hrl->hrk', query_heads.astype(jnp.float32), lift_denom.astype(jnp.float32), precision=largest_magnitude)
    state_list = []
    norm_list = []
    for prompt in range(PROMPTS):
        selected_rows = picks == prompt
        state_list.append(lax.optimization_barrier(jnp.sum(jnp.where(selected_rows[None, :, None, None], d_state, 0.0), axis=1)))
        norm_list.append(lax.optimization_barrier(jnp.sum(jnp.where(selected_rows[None, :, None], d_norm, 0.0), axis=1)))
    grad_low = jnp.stack(state_list, axis=1).astype(jnp.bfloat16)
    gnorm_low = jnp.stack(norm_list, axis=1).astype(jnp.bfloat16)
    grad_float = grad_low.astype(jnp.float32)
    gnorm_float = gnorm_low.astype(jnp.float32)

    def grad_step(carry, items):
        weight_rows, value_rows, rows_id, rows_member = items
        weight_single_precise = weight_rows.astype(jnp.float32)
        value_single_precise = value_rows.astype(jnp.float32)

        def single(unused):
            selected_entry = lax.dynamic_index_in_dim(grad_float, rows_id[0], 1, keepdims=False)
            selected_norm = lax.dynamic_index_in_dim(gnorm_float, rows_id[0], 1, keepdims=False)
            value_block_slice = jnp.einsum('noe,nec->noc', weight_single_precise, selected_entry, precision=largest_magnitude)
            key_block_slice = jnp.einsum('dje,dxe->djx', value_single_precise, selected_entry, precision=largest_magnitude) + selected_norm[:, None, :]
            return (key_block_slice, value_block_slice)

        def several(unused):
            spread = jnp.where(rows_member[None, :, :, None], weight_single_precise[:, :, None, :], 0.0)
            value_block_slice = jnp.einsum('htpk,hpkv->htv', spread, grad_float, precision=largest_magnitude)
            through = jnp.einsum('htv,hpkv->htpk', value_single_precise, grad_float, precision=largest_magnitude) + gnorm_float[:, None]
            key_block_slice = lax.optimization_barrier(jnp.sum(jnp.where(rows_member[None, :, :, None], through, 0.0), axis=2))
            return (key_block_slice, value_block_slice)
        return (carry, lax.cond(rows_id[0] == rows_id[-1], single, several, 0))
    unused_carry, grads_out = lax.scan(grad_step, 0, (weighted_blocks, value_blocks, id_blocks, member_blocks))
    key_blocks, value_blocks_out = grads_out
    key_grads = jnp.transpose(key_blocks, (1, 0, 2, 3)).reshape(MLSTM_HEADS, WINDOW_TOTAL, DK)
    value_grads = jnp.transpose(value_blocks_out, (1, 0, 2, 3)).reshape(MLSTM_HEADS, WINDOW_TOTAL, DV)
    key_grads = key_grads * weight[:, :, None]
    prompt_key_grad = jnp.transpose(key_grads, (1, 0, 2)).reshape(WINDOW_TOTAL, MLSTM_HEADS * DK).astype(jnp.bfloat16)
    prompt_value_grad = jnp.transpose(value_grads, (1, 0, 2)).reshape(WINDOW_TOTAL, MLSTM_HEADS * DV).astype(jnp.bfloat16)
    return (resp_out, prompt_key_grad, prompt_value_grad)
```

```python
import functools

import jax
import jax.numpy as jnp
from jax import lax
from jax.experimental import pallas as pl
from jax.experimental.pallas import tpu as pltpu
from jax.sharding import PartitionSpec as P

F32 = jnp.float32
BF16 = jnp.bfloat16
PROMPTS = 4
SEQ = 16
HEADS = 8
DK = 256
DV = 512
WIN = 1024
RLEN = 512
ROWS = DK // SEQ
AUX = 8
LANES = 128
SCALE = DK ** (-0.5)

VMEM = pl.BlockSpec(memory_space=pltpu.VMEM)
SMEM = pl.BlockSpec(memory_space=pltpu.SMEM)


def call(body, ins, outs, scratch, **kw):
    return pl.pallas_call(
        body,
        in_specs=ins,
        out_specs=tuple(VMEM for _ in outs),
        out_shape=tuple(jax.ShapeDtypeStruct(s, d) for s, d in outs),
        scratch_shapes=scratch,
        compiler_params=pltpu.CompilerParams(vmem_limit_bytes=48 << 20),
        **kw,
    )


def iota(shape, dim):
    return lax.broadcasted_iota(jnp.int32, shape, dim)


def ends_of(len_ref):
    e0 = len_ref[0]
    e1 = e0 + len_ref[1]
    e2 = e1 + len_ref[2]
    return e0, e1, e2


def prompt_at(position, ends):
    total = 0
    for e in ends:
        total = total + (position >= e).astype(jnp.int32)
    return total


def first_prompt(device, ends, slots):
    if slots == PROMPTS:
        return 0
    total = jnp.int32(0)
    for e in ends:
        total = total + jnp.where(device * WIN >= e, 1, 0)
    return total


def log_sigmoid(x):
    return jnp.minimum(x, 0.0) - jnp.log1p(jnp.exp(-jnp.abs(x)))


def dot(a, b, ca, cb):
    return lax.dot_general(a, b, (((ca,), (cb,)), ((), ())), preferred_element_type=F32)


def split_two(x):
    hi = x.astype(BF16)
    return hi, (x - hi.astype(F32)).astype(BF16)


def whole(x):
    return jnp.sum(jnp.sum(x, axis=0, keepdims=True), axis=1, keepdims=True)


def window_pid(me, ends):
    shape = (WIN // LANES, LANES)
    return prompt_at(me * WIN + iota(shape, 0) * LANES + iota(shape, 1), ends)


def state_kernel(slots, len_ref, pk, pv, pin, pf, msg, e_out, gates, inputs, wmat):
    me = lax.axis_index("seq")
    ends = ends_of(len_ref)
    groups = WIN // LANES
    for r in range(groups):
        gates[r : r + 1, :] = pf[:, r * LANES : (r + 1) * LANES]
        inputs[r : r + 1, :] = pin[:, r * LANES : (r + 1) * LANES]
    shape = (groups, LANES)
    pid = window_pid(me, ends)
    lane, row = iota(shape, 1), iota(shape, 0)
    lf = log_sigmoid(gates[...])
    tail = lf
    step = 1
    while step < LANES:
        tail = tail + jnp.where(lane < LANES - step, pltpu.roll(tail, LANES - step, 1), 0.0)
        step *= 2
    after = jnp.broadcast_to(tail[:, 0:1], shape)
    after = jnp.where(row < groups - 1, pltpu.roll(after, groups - 1, 0), 0.0)
    step = 1
    while step < groups:
        after = after + jnp.where(row < groups - step, pltpu.roll(after, groups - step, 0), 0.0)
        step *= 2
    sums = [whole(jnp.where(pid == p, lf, 0.0)) for p in range(PROMPTS)]
    later = jnp.where(
        pid == 0,
        sums[1] + sums[2] + sums[3],
        jnp.where(pid == 1, sums[2] + sums[3], jnp.where(pid == 2, sums[3], 0.0)),
    )
    expo = inputs[...] + ((tail - lf) + after - later)
    e_out[...] = expo
    weight = jnp.exp(expo)
    first = first_prompt(me, ends, slots)
    stacked = jnp.concatenate(
        [jnp.where(pid == first + s, weight, 0.0) for s in range(slots)], axis=0
    )
    if slots * groups < LANES:
        stacked = jnp.concatenate(
            [stacked, jnp.zeros((LANES - slots * groups, LANES), F32)], axis=0
        )
    columns = stacked.T
    for r in range(groups):
        rows = slice(r * LANES, (r + 1) * LANES)
        keys = pk[rows, :].astype(F32)
        for s in range(slots):
            at = s * groups + r
            wmat[s, rows, :] = (keys * columns[:, at : at + 1]).astype(BF16)
    for s in range(slots):
        state = dot(wmat[s], pv[...], 0, 0).astype(BF16)
        for dev in range(SEQ):
            msg[dev, s * ROWS : (s + 1) * ROWS, :] = state[dev * ROWS : (dev + 1) * ROWS, :]
    ashape = (AUX, DV)
    arow, alane = iota(ashape, 0), iota(ashape, 1)
    aux = jnp.zeros(ashape, F32)
    for p in range(PROMPTS):
        rest = jnp.broadcast_to(sums[p], ashape)
        for part in range(3):
            piece = rest.astype(BF16).astype(F32)
            aux = jnp.where((arow == 4 + part) & (alane == p), piece, aux)
            rest = rest - piece
    aux = aux.astype(BF16)
    for dev in range(SEQ):
        msg[dev, slots * ROWS : slots * ROWS + AUX, :] = aux


def spread_kernel(slots, len_ref, rp, m, expo, pk, out, aft, acc, low, afters):
    me = lax.axis_index("seq")
    ends = ends_of(len_ref)
    shape = (SEQ, LANES)
    lane, row = iota(shape, 1), iota(shape, 0)
    base = slots * ROWS
    gates = m[:, base : base + AUX, 0:LANES].astype(F32)
    sums = gates[:, 6, :] + gates[:, 5, :] + gates[:, 4, :]
    after = jnp.where(row < SEQ - 1, pltpu.roll(sums, SEQ - 1, 0), 0.0)
    step = 1
    while step < SEQ:
        after = after + jnp.where(row < SEQ - step, pltpu.roll(after, SEQ - step, 0), 0.0)
        step *= 2
    afters[...] = after
    mine = jnp.broadcast_to(afters[pl.ds(me, 1), :], aft.shape)
    aft[...] = mine
    factor = jnp.exp(after)
    if slots == PROMPTS:
        first = jnp.zeros(shape, jnp.int32)
    else:
        first = prompt_at(row * WIN, ends)
    acc[...] = jnp.zeros_like(acc)
    for s in range(slots):
        scale = jnp.sum(jnp.where(lane == first + s, factor, 0.0), axis=1, keepdims=True)
        for dev in range(SEQ):
            p = first_prompt(dev, ends, slots) + s
            f = scale[dev : dev + 1, :]
            acc[p] += f * m[dev, s * ROWS : (s + 1) * ROWS, :].astype(F32)
    for p in range(PROMPTS):
        low[p] = acc[p].astype(BF16)
    groups = WIN // LANES
    pid = window_pid(me, ends)
    rest = jnp.zeros((groups, LANES), F32)
    for p in range(PROMPTS):
        rest = jnp.where(pid == p, mine[0:1, p : p + 1], rest)
    weight = jnp.exp(expo[...] + rest)
    columns = jnp.concatenate([weight, jnp.zeros((LANES - groups, LANES), F32)], axis=0).T
    mrow = iota((8, LANES), 0)
    norms = jnp.zeros((8, DK), F32)
    for r in range(groups):
        weighted = pk[r * LANES : (r + 1) * LANES, :].astype(F32) * columns[:, r : r + 1]
        member = (jnp.broadcast_to(pid[r : r + 1, :], (8, LANES)) == mrow).astype(F32)
        norms = norms + dot(member.astype(BF16), weighted.astype(BF16), 1, 0)
    aux = jnp.zeros((AUX, DV), F32)
    arow = iota((AUX, DV), 0)
    for part, piece in enumerate(split_two(norms)):
        piece = piece.astype(F32)
        for pair in range(PROMPTS // 2):
            both = jnp.concatenate(
                [piece[2 * pair : 2 * pair + 1, :], piece[2 * pair + 1 : 2 * pair + 2, :]], axis=1
            )
            aux = jnp.where(arow == 2 * part + pair, both, aux)
    aux = aux.astype(BF16)
    for dev in range(SEQ):
        for r in range(2):
            out[dev, r * ROWS : (r + 1) * ROWS, :] = low[rp[2 * dev + r, 0]]
        out[dev, 2 * ROWS : 2 * ROWS + AUX, :] = aux


def respond_kernel(q, k, v, rin, rf, num, cols):
    shape = (8, RLEN)
    row, lane = iota(shape, 0), iota(shape, 1)
    gate = jnp.where(row == 0, rf[0, 0:1, :], rf[0, 1:2, :])
    cum = log_sigmoid(gate)
    step = 1
    while step < RLEN:
        cum = cum + jnp.where(lane >= step, pltpu.roll(cum, step, 1), 0.0)
        step *= 2
    tall = jnp.concatenate([cum, jnp.zeros((LANES - 8, RLEN), F32)], axis=0).T
    half = RLEN // 2
    clane = iota((RLEN, LANES), 1)
    packed = jnp.zeros((RLEN, LANES), F32)
    for r in range(2):
        ccol = tall[:, r : r + 1]
        srow = rin[0, r : r + 1, :] - cum[r : r + 1, :]
        for b in range(2):
            rows = slice(b * half, (b + 1) * half)
            width = (b + 1) * half
            scores = dot(q[r, rows, :], k[r, 0:width, :], 1, 1) * SCALE
            causal = iota((half, width), 0) + b * half >= iota((half, width), 1)
            decay = jnp.where(causal, ccol[rows, :] + srow[:, 0:width], -1e30)
            mixing = (scores * jnp.exp(decay)).astype(BF16)
            num[r, rows, :] = dot(mixing, v[r, 0:width, :], 1, 0)
            den = jnp.sum(mixing.astype(F32), axis=1, keepdims=True)
            cols[rows, :] = jnp.where(
                clane[rows, :] == r, den, packed[rows, :] if r == 0 else cols[rows, :]
            )
        lifted = jnp.exp(ccol) * SCALE
        cols[...] = jnp.where(clane == 2 + r, lifted, cols[...])


def hidden_kernel(rp, q, m, num, cols, og, gain, hid, cols2, msg, nrm):
    me = lax.axis_index("seq")
    aux = jnp.sum(m[:, 2 * ROWS : 2 * ROWS + AUX, :].astype(F32), axis=0)
    for p in range(PROMPTS):
        side = slice((p % 2) * DK, (p % 2 + 1) * DK)
        at = p // 2
        nrm[p : p + 1, :] = aux[at : at + 1, side] + aux[at + 2 : at + 3, side]
    clane = iota((RLEN, LANES), 1)
    sums = jnp.zeros((RLEN, LANES), F32)
    packed = jnp.zeros((RLEN, LANES), F32)
    for r in range(2):
        state = m[:, r * ROWS : (r + 1) * ROWS, :].reshape(DK, DV)
        norm = jnp.broadcast_to(nrm[pl.ds(rp[2 * me + r, 0], 1), :], (LANES, DK)).astype(BF16)
        lifted = cols[:, 2 + r : 3 + r]
        qn = dot(q[r], norm, 1, 1)[:, 0:1]
        den = cols[:, r : r + 1] + lifted * qn
        inverse = 1.0 / jnp.sqrt(den * den + 1.0)
        hidden = (num[r] + lifted * dot(q[r], state, 1, 0)) * inverse
        hid[r] = hidden
        squares = jnp.sum(hidden * hidden, axis=1, keepdims=True)
        dots = jnp.sum(og[r].astype(F32) * gain[...] * hidden, axis=1, keepdims=True)
        sums = jnp.where(clane == 2 * r, squares, jnp.where(clane == 2 * r + 1, dots, sums))
        lift = lifted * inverse
        ratio = lifted * den * (inverse * inverse)
        packed = jnp.where(clane == 4 + r, lift, jnp.where(clane == 6 + r, ratio, packed))
    cols2[...] = packed + sums
    rows = sums.T[0:8, :]
    for dev in range(HEADS):
        msg[dev] = rows


def grad_kernel(m, hid, cols2, og, gain, q, out, msg):
    total = m[0]
    for dev in range(1, HEADS):
        total = total + m[dev]
    features = HEADS * DV
    lists = []
    for r in range(2):
        inv = lax.rsqrt(total[2 * r : 2 * r + 1, :] / features + 1e-6)
        lists += [inv, total[2 * r + 1 : 2 * r + 2, :] * (inv * inv * inv) / features]
    rows = jnp.concatenate(lists + [jnp.zeros((LANES - 4, RLEN), F32)], axis=0)
    tall = rows.T
    norms = []
    for r in range(2):
        inv, coef = tall[:, 2 * r : 2 * r + 1], tall[:, 2 * r + 1 : 2 * r + 2]
        squares, dots = cols2[:, 2 * r : 2 * r + 1], cols2[:, 2 * r + 1 : 2 * r + 2]
        lift, ratio = cols2[:, 4 + r : 5 + r], cols2[:, 6 + r : 7 + r]
        hidden = hid[r]
        out[r] = (hidden * gain[...] * inv).astype(BF16)
        d_hidden = gain[...] * og[r].astype(F32) * inv - hidden * coef
        lift_numer = (lift * d_hidden).astype(BF16)
        lift_denom = (-(inv * dots - coef * squares) * ratio).astype(BF16).astype(F32)
        state = dot(q[r], lift_numer, 0, 0).astype(BF16)
        for dev in range(SEQ):
            msg[dev, r * ROWS : (r + 1) * ROWS, :] = state[dev * ROWS : (dev + 1) * ROWS, :]
        norms.append(split_two(jnp.sum(lift_denom * q[r].astype(F32), axis=0, keepdims=True)))
    arow = iota((AUX, DV), 0)
    aux = jnp.zeros((AUX, DV), F32)
    for part in range(2):
        both = jnp.concatenate([norms[0][part], norms[1][part]], axis=1).astype(F32)
        aux = jnp.where(arow == part, both, aux)
    aux = aux.astype(BF16)
    for dev in range(SEQ):
        msg[dev, 2 * ROWS : 2 * ROWS + AUX, :] = aux


def gather_kernel(slots, len_ref, rp, m, out, gn, acc, aacc, low):
    ends = ends_of(len_ref)
    acc[...] = jnp.zeros_like(acc)
    aacc[...] = jnp.zeros_like(aacc)
    for dev in range(SEQ):
        for r in range(2):
            p = rp[2 * dev + r, 0]
            acc[p] += m[dev, r * ROWS : (r + 1) * ROWS, :].astype(F32)
            aacc[r, p] += m[dev, 2 * ROWS : 2 * ROWS + AUX, :].astype(F32)
    for p in range(PROMPTS):
        low[p] = acc[p].astype(BF16)
        total = jnp.zeros((1, DK), F32)
        for r in range(2):
            cols = slice(r * DK, (r + 1) * DK)
            total = total + (aacc[r, p, 0:1, cols] + aacc[r, p, 1:2, cols])
        gn[p : p + 1, :] = total.astype(BF16).astype(F32)
    gn[PROMPTS:, :] = jnp.zeros((8 - PROMPTS, DK), F32)
    for dev in range(SEQ):
        first = first_prompt(dev, ends, slots)
        for s in range(slots):
            out[dev, s * ROWS : (s + 1) * ROWS, :] = low[jnp.minimum(first + s, PROMPTS - 1)]


def prompt_kernel(slots, len_ref, m, gn, expo, aft, pk, pv, kg, vg):
    me = lax.axis_index("seq")
    ends = ends_of(len_ref)
    groups = WIN // LANES
    pid = window_pid(me, ends)
    after = jnp.zeros((groups, LANES), F32)
    for p in range(PROMPTS):
        after = jnp.where(pid == p, aft[0:1, p : p + 1], after)
    weight = jnp.exp(expo[...] + after)
    first = first_prompt(me, ends, slots)
    stacked = jnp.concatenate(
        [jnp.where(pid == first + s, weight, 0.0) for s in range(slots)], axis=0
    )
    if slots * groups < LANES:
        stacked = jnp.concatenate(
            [stacked, jnp.zeros((LANES - slots * groups, LANES), F32)], axis=0
        )
    columns = stacked.T
    grads = [m[:, s * ROWS : (s + 1) * ROWS, :].reshape(DK, DV) for s in range(slots)]
    norms = [gn[pl.ds(jnp.minimum(first + s, PROMPTS - 1), 1), :] for s in range(slots)]
    for r in range(groups):
        rows = slice(r * LANES, (r + 1) * LANES)
        keys = pk[rows, :].astype(F32)
        values = pv[rows, :]
        key_grad = jnp.zeros((LANES, DK), F32)
        value_grad = jnp.zeros((LANES, DV), F32)
        for s in range(slots):
            w = columns[:, s * groups + r : s * groups + r + 1]
            value_grad = value_grad + dot((keys * w).astype(BF16), grads[s], 1, 0)
            key_grad = key_grad + w * (dot(values, grads[s], 1, 1) + norms[s])
        kg[rows, :] = key_grad.astype(BF16)
        vg[rows, :] = value_grad.astype(BF16)


def exchange(x, axis):
    return lax.all_to_all(x, axis, 0, 0, tiled=True)


def step(slots, pk, pv, pin, pf, lengths, rp, q, k, v, rin, rf, gain, og):
    groups = WIN // LANES
    part = functools.partial
    msg1, expo = call(
        part(state_kernel, slots),
        [SMEM] + [VMEM] * 4,
        [((SEQ, slots * ROWS + AUX, DV), BF16), ((groups, LANES), F32)],
        [
            pltpu.VMEM((groups, LANES), F32),
            pltpu.VMEM((groups, LANES), F32),
            pltpu.VMEM((slots, WIN, DK), BF16),
        ],
        name="state_kernel",
    )(lengths, pk, pv, pin, pf)
    got1 = exchange(msg1, "seq")
    num, cols = call(
        respond_kernel,
        [VMEM] * 5,
        [((2, RLEN, DV), F32), ((RLEN, LANES), F32)],
        [],
        name="respond_kernel",
    )(q, k, v, rin, rf)
    msg2, aft = call(
        part(spread_kernel, slots),
        [SMEM, SMEM] + [VMEM] * 3,
        [((SEQ, 2 * ROWS + AUX, DV), BF16), ((8, LANES), F32)],
        [
            pltpu.VMEM((PROMPTS + slots, ROWS, DV), F32),
            pltpu.VMEM((PROMPTS, ROWS, DV), BF16),
            pltpu.VMEM((SEQ, LANES), F32),
        ],
        name="spread_kernel",
    )(lengths, rp, got1, expo, pk)
    got2 = exchange(msg2, "seq")
    hid, cols2, msg3 = call(
        hidden_kernel,
        [SMEM] + [VMEM] * 6,
        [((2, RLEN, DV), F32), ((RLEN, LANES), F32), ((HEADS, 8, RLEN), F32)],
        [pltpu.VMEM((8, DK), F32)],
        name="hidden_kernel",
    )(rp, q, got2, num, cols, og, gain)
    got3 = exchange(msg3, "head")
    resp_out, msg4 = call(
        grad_kernel,
        [VMEM] * 6,
        [((2, RLEN, DV), BF16), ((SEQ, 2 * ROWS + AUX, DV), BF16)],
        [],
        name="grad_kernel",
    )(got3, hid, cols2, og, gain, q)
    got4 = exchange(msg4, "seq")
    msg5, gn = call(
        part(gather_kernel, slots),
        [SMEM, SMEM, VMEM],
        [((SEQ, slots * ROWS, DV), BF16), ((8, DK), F32)],
        [
            pltpu.VMEM((PROMPTS, ROWS, DV), F32),
            pltpu.VMEM((2, PROMPTS, AUX, DV), F32),
            pltpu.VMEM((PROMPTS, ROWS, DV), BF16),
        ],
        name="gather_kernel",
    )(lengths, rp, got4)
    got5 = exchange(msg5, "seq")
    key_grad, value_grad = call(
        part(prompt_kernel, slots),
        [SMEM] + [VMEM] * 6,
        [((WIN, DK), BF16), ((WIN, DV), BF16)],
        [],
        name="prompt_kernel",
    )(lengths, got5, gn, expo, aft, pk, pv)
    return resp_out, key_grad, value_grad


def local(pk, pv, pin, pf, lengths, rp, q, k, v, rin, rf, gain, og):
    return step(4, pk, pv, pin, pf, lengths, rp, q, k, v, rin, rf, gain.reshape(1, DV), og)


def solution(mesh):
    in_specs = (
        P("seq", "head"),
        P("seq", "head"),
        P("head", "seq"),
        P("head", "seq"),
        P(),
        P(),
        P("seq", None, "head"),
        P("seq", None, "head"),
        P("seq", None, "head"),
        P("head", "seq", None),
        P("head", "seq", None),
        P("head"),
        P("seq", None, "head"),
    )
    out_specs = (P("seq", None, "head"), P("seq", "head"), P("seq", "head"))
    return jax.shard_map(local, mesh=mesh, in_specs=in_specs, out_specs=out_specs, check_vma=False)
```

```python
import functools

import jax
import jax.numpy as jnp
from jax import lax
from jax.experimental import pallas as pl
from jax.experimental.pallas import tpu as pltpu
from jax.sharding import PartitionSpec as P

F32 = jnp.float32
BF16 = jnp.bfloat16
PROMPTS = 4
SEQ = 16
HEADS = 8
DK = 256
DV = 512
WIN = 1024
RLEN = 512
ROWS = DK // SEQ
LANES = 128
TILES = DV // LANES
STATE = ROWS * TILES
AUX = 8
NAUX = 16
GROUP = 256
SCALE = DK ** (-0.5)

VMEM = pl.BlockSpec(memory_space=pltpu.VMEM)
SMEM = pl.BlockSpec(memory_space=pltpu.SMEM)
HBM = pl.BlockSpec(memory_space=pltpu.HBM)
ANY = pl.BlockSpec(memory_space=pl.ANY)


def call(body, ins, outs, scratch, spec=VMEM, **kw):
    return pl.pallas_call(
        body,
        in_specs=ins,
        out_specs=tuple(spec for _ in outs),
        out_shape=tuple(jax.ShapeDtypeStruct(s, d) for s, d in outs),
        scratch_shapes=scratch,
        compiler_params=pltpu.CompilerParams(vmem_limit_bytes=24 << 20),
        **kw,
    )


def iota(shape, dim):
    return lax.broadcasted_iota(jnp.int32, shape, dim)


def ends_of(len_ref):
    e0 = len_ref[0]
    e1 = e0 + len_ref[1]
    e2 = e1 + len_ref[2]
    return e0, e1, e2


def prompt_at(position, ends):
    total = 0
    for e in ends:
        total = total + (position >= e).astype(jnp.int32)
    return total


def first_prompt(device, ends, slots):
    if slots == PROMPTS:
        return 0
    total = jnp.int32(0)
    for e in ends:
        total = total + jnp.where(device * WIN >= e, 1, 0)
    return total


def log_sigmoid(x):
    return jnp.minimum(x, 0.0) - jnp.log1p(jnp.exp(-jnp.abs(x)))


def dot(a, b, ca, cb):
    return lax.dot_general(a, b, (((ca,), (cb,)), ((), ())), preferred_element_type=F32)


def split_two(x):
    hi = x.astype(BF16)
    return hi, (x - hi.astype(F32)).astype(BF16)


def send_state(msg, dev, slot, rows):
    for c in range(TILES):
        at = slot * STATE + c * ROWS
        msg[dev, at : at + ROWS, :] = rows[:, c * LANES : (c + 1) * LANES]


def received(m, slot):
    tiles = []
    for c in range(TILES):
        start = slot * STATE + c * ROWS
        if not isinstance(start, int):
            start = pl.multiple_of(start, ROWS)
        tiles.append(m[:, pl.ds(start, ROWS), :].reshape(DK, LANES))
    return jnp.concatenate(tiles, axis=1)


def whole(x):
    return jnp.sum(jnp.sum(x, axis=0, keepdims=True), axis=1, keepdims=True)


def window_pid(me, ends):
    shape = (WIN // LANES, LANES)
    return prompt_at(me * WIN + iota(shape, 0) * LANES + iota(shape, 1), ends)


def state_kernel(
    slots, len_hbm, pk_hbm, pv_hbm, pin_hbm, pf_hbm, msg, e_out, len_ref, gates, inputs, pk, pv, wmat, sems
):
    me = lax.axis_index("seq")
    groups = WIN // LANES
    copies = [
        pltpu.make_async_copy(len_hbm, len_ref, sems.at[0]),
        pltpu.make_async_copy(pf_hbm, gates, sems.at[1]),
        pltpu.make_async_copy(pin_hbm, inputs, sems.at[2]),
        pltpu.make_async_copy(pk_hbm, pk, sems.at[3]),
        pltpu.make_async_copy(pv_hbm, pv, sems.at[4]),
    ]
    for copy in copies:
        copy.start()
    for copy in copies[:3]:
        copy.wait()
    ends = ends_of(len_ref)
    shape = (groups, LANES)
    pid = window_pid(me, ends)
    lane, row = iota(shape, 1), iota(shape, 0)

    def folded(ref):
        return jnp.concatenate(
            [ref[:, r * LANES : (r + 1) * LANES] for r in range(groups)], axis=0
        )

    lf = log_sigmoid(folded(gates))
    tail = lf
    step = 1
    while step < LANES:
        tail = tail + jnp.where(lane < LANES - step, pltpu.roll(tail, LANES - step, 1), 0.0)
        step *= 2
    after = jnp.broadcast_to(tail[:, 0:1], shape)
    after = jnp.where(row < groups - 1, pltpu.roll(after, groups - 1, 0), 0.0)
    step = 1
    while step < groups:
        after = after + jnp.where(row < groups - step, pltpu.roll(after, groups - step, 0), 0.0)
        step *= 2
    sums = [whole(jnp.where(pid == p, lf, 0.0)) for p in range(PROMPTS)]
    later = jnp.where(
        pid == 0,
        sums[1] + sums[2] + sums[3],
        jnp.where(pid == 1, sums[2] + sums[3], jnp.where(pid == 2, sums[3], 0.0)),
    )
    expo = folded(inputs) + ((tail - lf) + after - later)
    e_out[...] = expo
    weight = jnp.exp(expo)
    first = first_prompt(me, ends, slots)
    stacked = jnp.concatenate(
        [jnp.where(pid == first + s, weight, 0.0) for s in range(slots)]
        + [jnp.zeros((LANES - slots * groups, LANES), F32)],
        axis=0,
    )
    columns = stacked.T
    ashape = (AUX, LANES)
    arow, alane = iota(ashape, 0), iota(ashape, 1)
    aux = jnp.zeros(ashape, F32)
    for p in range(PROMPTS):
        rest = jnp.broadcast_to(sums[p], ashape)
        for part in range(3):
            piece = rest.astype(BF16).astype(F32)
            aux = jnp.where((arow == part) & (alane == p), piece, aux)
            rest = rest - piece
    aux = aux.astype(BF16)
    for dev in range(SEQ):
        msg[dev, slots * STATE : slots * STATE + AUX, :] = aux
    copies[3].wait()
    for r in range(groups):
        rows = slice(r * LANES, (r + 1) * LANES)
        keys = pk[rows, :].astype(F32)
        for s in range(slots):
            at = s * groups + r
            wmat[s, rows, :] = (keys * columns[:, at : at + 1]).astype(BF16)
    copies[4].wait()
    for s in range(slots):
        state = dot(wmat[s], pv[...], 0, 0).astype(BF16)
        for dev in range(SEQ):
            send_state(msg, dev, s, state[dev * ROWS : (dev + 1) * ROWS, :])


def spread_kernel(slots, len_ref, rp, m, expo, pk, unused, out, aft, acc, low, afters):
    me = lax.axis_index("seq")
    ends = ends_of(len_ref)
    shape = (SEQ, LANES)
    lane, row = iota(shape, 1), iota(shape, 0)
    base = slots * STATE
    gates = m[:, base : base + AUX, :].astype(F32)
    sums = gates[:, 2, :] + gates[:, 1, :] + gates[:, 0, :]
    after = jnp.where(row < SEQ - 1, pltpu.roll(sums, SEQ - 1, 0), 0.0)
    step = 1
    while step < SEQ:
        after = after + jnp.where(row < SEQ - step, pltpu.roll(after, SEQ - step, 0), 0.0)
        step *= 2
    afters[...] = after
    mine = jnp.broadcast_to(afters[pl.ds(me, 1), :], aft.shape)
    aft[...] = mine
    factor = jnp.exp(after)
    if slots == PROMPTS:
        first = jnp.zeros(shape, jnp.int32)
    else:
        first = prompt_at(row * WIN, ends)
    acc[...] = jnp.zeros_like(acc)
    for s in range(slots):
        scale = jnp.sum(jnp.where(lane == first + s, factor, 0.0), axis=1, keepdims=True)
        for dev in range(SEQ):
            p = first_prompt(dev, ends, slots) + s
            f = scale[dev : dev + 1, :]
            acc[p] += f * m[dev, s * STATE : (s + 1) * STATE, :].astype(F32)
    for p in range(PROMPTS):
        low[p] = acc[p].astype(BF16)
    groups = WIN // LANES
    pid = window_pid(me, ends)
    rest = jnp.zeros((groups, LANES), F32)
    for p in range(PROMPTS):
        rest = jnp.where(pid == p, mine[0:1, p : p + 1], rest)
    weight = jnp.exp(expo[...] + rest)
    columns = jnp.concatenate([weight, jnp.zeros((LANES - groups, LANES), F32)], axis=0).T
    mrow = iota((8, LANES), 0)
    norms = jnp.zeros((8, DK), F32)
    for r in range(groups):
        weighted = pk[r * LANES : (r + 1) * LANES, :].astype(F32) * columns[:, r : r + 1]
        member = (jnp.broadcast_to(pid[r : r + 1, :], (8, LANES)) == mrow).astype(F32)
        norms = norms + dot(member.astype(BF16), weighted.astype(BF16), 1, 0)
    aux = []
    for piece in split_two(norms):
        piece = piece.astype(F32)
        aux += [piece[0:PROMPTS, 0:LANES], piece[0:PROMPTS, LANES:DK]]
    aux = jnp.concatenate(aux, axis=0).astype(BF16)
    for dev in range(SEQ):
        for r in range(2):
            out[dev, r * STATE : (r + 1) * STATE, :] = low[rp[2 * dev + r, 0]]
        out[dev, 2 * STATE : 2 * STATE + NAUX, :] = aux


def respond_kernel(q, k, v, rin, rf, num, cols):
    shape = (8, RLEN)
    row, lane = iota(shape, 0), iota(shape, 1)
    gate = jnp.where(row == 0, rf[0, 0:1, :], rf[0, 1:2, :])
    cum = log_sigmoid(gate)
    step = 1
    while step < RLEN:
        cum = cum + jnp.where(lane >= step, pltpu.roll(cum, step, 1), 0.0)
        step *= 2
    tall = jnp.concatenate([cum, jnp.zeros((LANES - 8, RLEN), F32)], axis=0).T
    half = RLEN // 2
    clane = iota((RLEN, LANES), 1)
    packed = jnp.zeros((RLEN, LANES), F32)
    for r in range(2):
        ccol = tall[:, r : r + 1]
        srow = rin[0, r : r + 1, :] - cum[r : r + 1, :]
        for b in range(2):
            rows = slice(b * half, (b + 1) * half)
            width = (b + 1) * half
            scores = dot(q[r, rows, :], k[r, 0:width, :], 1, 1) * SCALE
            causal = iota((half, width), 0) + b * half >= iota((half, width), 1)
            decay = jnp.where(causal, ccol[rows, :] + srow[:, 0:width], -1e30)
            mixing = (scores * jnp.exp(decay)).astype(BF16)
            num[r, rows, :] = dot(mixing, v[r, 0:width, :], 1, 0)
            den = jnp.sum(mixing.astype(F32), axis=1, keepdims=True)
            cols[rows, :] = jnp.where(
                clane[rows, :] == r, den, packed[rows, :] if r == 0 else cols[rows, :]
            )
        lifted = jnp.exp(ccol) * SCALE
        cols[...] = jnp.where(clane == 2 + r, lifted, cols[...])


def hidden_kernel(rp, q, m, num, cols, og, gain, hid, cols2, msg, nrm):
    me = lax.axis_index("seq")
    aux = jnp.sum(m[:, 2 * STATE : 2 * STATE + NAUX, :].astype(F32), axis=0)
    aux = aux[0:8, :] + aux[8:16, :]
    nrm[0:PROMPTS, :] = jnp.concatenate([aux[0:PROMPTS, :], aux[PROMPTS:8, :]], axis=1)
    clane = iota((RLEN, LANES), 1)
    sums = jnp.zeros((RLEN, LANES), F32)
    packed = jnp.zeros((RLEN, LANES), F32)
    for r in range(2):
        norm = jnp.broadcast_to(nrm[pl.ds(rp[2 * me + r, 0], 1), :], (LANES, DK)).astype(BF16)
        lifted = cols[:, 2 + r : 3 + r]
        qn = dot(q[r], norm, 1, 1)[:, 0:1]
        den = cols[:, r : r + 1] + lifted * qn
        inverse = lax.rsqrt(den * den + 1.0)
        hidden = (num[r] + lifted * dot(q[r], received(m, r), 1, 0)) * inverse
        hid[r] = hidden
        squares = jnp.sum(hidden * hidden, axis=1, keepdims=True)
        dots = jnp.sum(og[r].astype(F32) * gain[...] * hidden, axis=1, keepdims=True)
        sums = jnp.where(clane == 2 * r, squares, jnp.where(clane == 2 * r + 1, dots, sums))
        lift = lifted * inverse
        ratio = lifted * den * (inverse * inverse)
        packed = jnp.where(clane == 4 + r, lift, jnp.where(clane == 6 + r, ratio, packed))
    cols2[...] = packed + sums
    rows = sums.T
    rows = jnp.concatenate(
        [rows[0:4, c * LANES : (c + 1) * LANES] for c in range(RLEN // LANES)], axis=0
    )
    for dev in range(HEADS):
        msg[dev] = rows


def grad_kernel(m, hid, cols2, og, gain, q, out, msg, numer, denom):
    total = m[0]
    for dev in range(1, HEADS):
        total = total + m[dev]
    features = HEADS * DV
    total = jnp.concatenate([total, jnp.zeros((LANES - 16, LANES), F32)], axis=0).T
    inverses = lax.rsqrt(total / features + 1e-6)
    coefs = pltpu.roll(total, LANES - 1, 1) * (inverses * inverses * inverses) / features
    rows8 = []
    for r in range(2):
        for c in range(RLEN // LANES):
            rows = slice(c * LANES, (c + 1) * LANES)
            at = 4 * c + 2 * r
            inv, coef = inverses[:, at : at + 1], coefs[:, at : at + 1]
            small = cols2[rows, :]
            squares, dots = small[:, 2 * r : 2 * r + 1], small[:, 2 * r + 1 : 2 * r + 2]
            lift, ratio = small[:, 4 + r : 5 + r], small[:, 6 + r : 7 + r]
            hidden = hid[r, rows, :]
            scaled = gain[...] * inv
            out[r, rows, :] = (hidden * scaled).astype(BF16)
            d_hidden = scaled * og[r, rows, :].astype(F32) - hidden * coef
            numer[rows, :] = (lift * d_hidden).astype(BF16)
            lift_denom = (-(inv * dots - coef * squares) * ratio).astype(BF16).astype(F32)
            part = jnp.sum(lift_denom * q[r, rows, :].astype(F32), axis=0, keepdims=True)
            denom[...] = part if c == 0 else denom[...] + part
        state = dot(q[r], numer[...], 0, 0).astype(BF16)
        for dev in range(SEQ):
            send_state(msg, dev, r, state[dev * ROWS : (dev + 1) * ROWS, :])
        for piece in split_two(denom[...]):
            piece = piece.astype(F32)
            rows8 += [piece[:, 0:LANES], piece[:, LANES:DK]]
    aux = jnp.concatenate(rows8, axis=0).astype(BF16)
    for dev in range(SEQ):
        msg[dev, 2 * STATE : 2 * STATE + AUX, :] = aux


def gather_kernel(slots, len_ref, rp, m, out, gn, acc, aacc, low):
    ends = ends_of(len_ref)
    acc[...] = jnp.zeros_like(acc)
    aacc[...] = jnp.zeros_like(aacc)
    for dev in range(SEQ):
        for r in range(2):
            p = rp[2 * dev + r, 0]
            acc[p] += m[dev, r * STATE : (r + 1) * STATE, :].astype(F32)
            aacc[r, p] += m[dev, 2 * STATE : 2 * STATE + AUX, :].astype(F32)
    for p in range(PROMPTS):
        low[p] = acc[p].astype(BF16)
        total = jnp.zeros((2, LANES), F32)
        for r in range(2):
            total = total + (aacc[r, p, 4 * r : 4 * r + 2, :] + aacc[r, p, 4 * r + 2 : 4 * r + 4, :])
        total = total.astype(BF16).astype(F32)
        gn[p : p + 1, :] = jnp.concatenate([total[0:1, :], total[1:2, :]], axis=1)
    gn[PROMPTS:, :] = jnp.zeros((8 - PROMPTS, DK), F32)
    for dev in range(SEQ):
        first = first_prompt(dev, ends, slots)
        for s in range(slots):
            out[dev, s * STATE : (s + 1) * STATE, :] = low[jnp.minimum(first + s, PROMPTS - 1)]


def prompt_kernel(slots, len_ref, m, gn, expo, aft, pk, pv, kg_hbm, vg_hbm, kg, vg, sems):
    me = lax.axis_index("seq")
    ends = ends_of(len_ref)
    groups = WIN // LANES
    pid = window_pid(me, ends)
    after = jnp.zeros((groups, LANES), F32)
    for p in range(PROMPTS):
        after = jnp.where(pid == p, aft[0:1, p : p + 1], after)
    weight = jnp.exp(expo[...] + after)
    first = first_prompt(me, ends, slots)
    stacked = jnp.concatenate(
        [weight, pid.astype(F32), jnp.zeros((LANES - 2 * groups, LANES), F32)], axis=0
    )
    columns = stacked.T

    def at_row(j):
        total = jnp.int32(0)
        for e in ends:
            total = total + jnp.where(me * WIN + j >= e, 1, 0)
        return total

    copies = []
    per = GROUP // LANES
    for g in range(WIN // GROUP):
        rows = slice(g * GROUP, (g + 1) * GROUP)
        w, ids = (
            jnp.concatenate(
                [columns[:, at + g * per + i : at + g * per + i + 1] for i in range(per)], axis=0
            )
            for at in (0, groups)
        )
        weighted = (pk[rows, :].astype(F32) * w).astype(BF16)
        low, high = at_row(g * GROUP), at_row((g + 1) * GROUP - 1)

        def grads(p):
            grad = received(m, p - first)
            value_grad = dot(weighted, grad, 1, 0)
            key_grad = w * (dot(pv[rows, :], grad, 1, 1) + gn[pl.ds(p, 1), :])
            return key_grad.astype(BF16), value_grad.astype(BF16)

        kg[rows, :], vg[rows, :] = grads(low)

        @pl.loop(low + 1, high + 1)
        def _(p):
            key_grad, value_grad = grads(p)
            mine = ids == p.astype(F32)
            kg[rows, :] = jnp.where(mine, key_grad, kg[rows, :])
            vg[rows, :] = jnp.where(mine, value_grad, vg[rows, :])

        copies += [
            pltpu.make_async_copy(kg.at[rows], kg_hbm.at[rows], sems.at[2 * g]),
            pltpu.make_async_copy(vg.at[rows], vg_hbm.at[rows], sems.at[2 * g + 1]),
        ]
        for copy in copies[-2:]:
            copy.start()
    for copy in copies:
        copy.wait()


def exchange(x, axis):
    return lax.all_to_all(x, axis, 0, 0, tiled=True)


def step(slots, pk, pv, pin, pf, lengths, rp, q, k, v, rin, rf, gain, og):
    groups = WIN // LANES
    part = functools.partial
    msg1, expo = call(
        part(state_kernel, slots),
        [HBM] * 5,
        [((SEQ, slots * STATE + AUX, LANES), BF16), ((groups, LANES), F32)],
        [
            pltpu.SMEM((PROMPTS,), jnp.int32),
            pltpu.VMEM((1, WIN), F32),
            pltpu.VMEM((1, WIN), F32),
            pltpu.VMEM((WIN, DK), BF16),
            pltpu.VMEM((WIN, DV), BF16),
            pltpu.VMEM((slots, WIN, DK), BF16),
            pltpu.SemaphoreType.DMA((5,)),
        ],
        name="state_kernel",
    )(lengths, pk, pv, pin, pf)
    got1 = exchange(msg1, "seq")
    num, cols = call(
        respond_kernel,
        [VMEM] * 5,
        [((2, RLEN, DV), F32), ((RLEN, LANES), F32)],
        [],
        name="respond_kernel",
    )(q, k, v, rin, rf)
    msg2, aft = call(
        part(spread_kernel, slots),
        [SMEM, SMEM] + [VMEM] * 3 + [ANY],
        [((SEQ, 2 * STATE + NAUX, LANES), BF16), ((8, LANES), F32)],
        [
            pltpu.VMEM((PROMPTS + slots, STATE, LANES), F32),
            pltpu.VMEM((PROMPTS, STATE, LANES), BF16),
            pltpu.VMEM((SEQ, LANES), F32),
        ],
        name="spread_kernel",
    )(lengths, rp, got1, expo, pk, cols)
    got2 = exchange(msg2, "seq")
    hid, cols2, msg3 = call(
        hidden_kernel,
        [SMEM] + [VMEM] * 6,
        [((2, RLEN, DV), F32), ((RLEN, LANES), F32), ((HEADS, 16, LANES), F32)],
        [pltpu.VMEM((8, DK), F32)],
        name="hidden_kernel",
    )(rp, q, got2, num, cols, og, gain)
    got3 = exchange(msg3, "head")
    resp_out, msg4 = call(
        grad_kernel,
        [VMEM] * 6,
        [((2, RLEN, DV), BF16), ((SEQ, 2 * STATE + AUX, LANES), BF16)],
        [pltpu.VMEM((RLEN, DV), BF16), pltpu.VMEM((1, DK), F32)],
        name="grad_kernel",
    )(got3, hid, cols2, og, gain, q)
    got4 = exchange(msg4, "seq")
    msg5, gn = call(
        part(gather_kernel, slots),
        [SMEM, SMEM, VMEM],
        [((SEQ, slots * STATE, LANES), BF16), ((8, DK), F32)],
        [
            pltpu.VMEM((PROMPTS, STATE, LANES), F32),
            pltpu.VMEM((2, PROMPTS, AUX, LANES), F32),
            pltpu.VMEM((PROMPTS, STATE, LANES), BF16),
        ],
        name="gather_kernel",
    )(lengths, rp, got4)
    got5 = exchange(msg5, "seq")
    key_grad, value_grad = call(
        part(prompt_kernel, slots),
        [SMEM] + [VMEM] * 6,
        [((WIN, DK), BF16), ((WIN, DV), BF16)],
        [
            pltpu.VMEM((WIN, DK), BF16),
            pltpu.VMEM((WIN, DV), BF16),
            pltpu.SemaphoreType.DMA((2 * WIN // GROUP,)),
        ],
        spec=HBM,
        name="prompt_kernel",
    )(lengths, got5, gn, expo, aft, pk, pv)
    return resp_out, key_grad, value_grad


def local(pk, pv, pin, pf, lengths, rp, q, k, v, rin, rf, gain, og):
    e0 = lengths[0]
    e1 = e0 + lengths[1]
    e2 = e1 + lengths[2]
    crowded = ((e0 // WIN == e1 // WIN) & (e0 % WIN != 0)) | ((e1 // WIN == e2 // WIN) & (e1 % WIN != 0))
    args = (pk, pv, pin, pf, lengths, rp, q, k, v, rin, rf, gain.reshape(1, DV), og)
    return lax.cond(
        crowded, functools.partial(step, PROMPTS), functools.partial(step, 2), *args
    )


def solution(mesh):
    in_specs = (
        P("seq", "head"),
        P("seq", "head"),
        P("head", "seq"),
        P("head", "seq"),
        P(),
        P(),
        P("seq", None, "head"),
        P("seq", None, "head"),
        P("seq", None, "head"),
        P("head", "seq", None),
        P("head", "seq", None),
        P("head"),
        P("seq", None, "head"),
    )
    out_specs = (P("seq", None, "head"), P("seq", "head"), P("seq", "head"))
    return jax.shard_map(local, mesh=mesh, in_specs=in_specs, out_specs=out_specs, check_vma=False)
```

```python
import functools

import jax
import jax.numpy as jnp
from jax import lax
from jax.experimental import pallas as pl
from jax.experimental.pallas import tpu as pltpu
from jax.sharding import PartitionSpec as P

F32 = jnp.float32
BF16 = jnp.bfloat16
PROMPTS = 4
SEQ = 16
HEADS = 8
DK = 256
DV = 512
WIN = 1024
RLEN = 512
ROWS = DK // SEQ
LANES = 128
TILES = DV // LANES
STATE = ROWS * TILES
AUX = 8
NAUX = 16
GROUP = 256
SCALE = DK ** (-0.5)

VMEM = pl.BlockSpec(memory_space=pltpu.VMEM)
SMEM = pl.BlockSpec(memory_space=pltpu.SMEM)
HBM = pl.BlockSpec(memory_space=pltpu.HBM)
ANY = pl.BlockSpec(memory_space=pl.ANY)


def call(body, ins, outs, scratch, spec=VMEM, **kw):
    return pl.pallas_call(
        body,
        in_specs=ins,
        out_specs=spec if isinstance(spec, tuple) else tuple(spec for _ in outs),
        out_shape=tuple(jax.ShapeDtypeStruct(s, d) for s, d in outs),
        scratch_shapes=scratch,
        compiler_params=pltpu.CompilerParams(vmem_limit_bytes=24 << 20),
        **kw,
    )


def iota(shape, dim):
    return lax.broadcasted_iota(jnp.int32, shape, dim)


def ends_of(len_ref):
    e0 = len_ref[0]
    e1 = e0 + len_ref[1]
    e2 = e1 + len_ref[2]
    return e0, e1, e2


def prompt_at(position, ends):
    total = 0
    for e in ends:
        total = total + (position >= e).astype(jnp.int32)
    return total


def first_prompt(device, ends, slots):
    if slots == PROMPTS:
        return 0
    total = jnp.int32(0)
    for e in ends:
        total = total + jnp.where(device * WIN >= e, 1, 0)
    return total


def log_sigmoid(x):
    return jnp.minimum(x, 0.0) - jnp.log1p(jnp.exp(-jnp.abs(x)))


def dot(a, b, ca, cb):
    return lax.dot_general(a, b, (((ca,), (cb,)), ((), ())), preferred_element_type=F32)


def split_two(x):
    hi = x.astype(BF16)
    return hi, (x - hi.astype(F32)).astype(BF16)


def send_state(msg, dev, slot, rows):
    for c in range(TILES):
        at = slot * STATE + c * ROWS
        msg[dev, at : at + ROWS, :] = rows[:, c * LANES : (c + 1) * LANES]


def received(m, slot):
    tiles = []
    for c in range(TILES):
        start = slot * STATE + c * ROWS
        if not isinstance(start, int):
            start = pl.multiple_of(start, ROWS)
        tiles.append(m[:, pl.ds(start, ROWS), :].reshape(DK, LANES))
    return jnp.concatenate(tiles, axis=1)


def whole(x):
    return jnp.sum(jnp.sum(x, axis=0, keepdims=True), axis=1, keepdims=True)


def window_pid(me, ends):
    shape = (WIN // LANES, LANES)
    return prompt_at(me * WIN + iota(shape, 0) * LANES + iota(shape, 1), ends)


def state_kernel(
    slots, len_hbm, pk_hbm, pv_hbm, pin_hbm, pf_hbm, msg, e_out, flag, len_ref, gates, inputs, pk, pv, wmat, sems
):
    me = lax.axis_index("seq")
    groups = WIN // LANES
    copies = [
        pltpu.make_async_copy(len_hbm, len_ref, sems.at[0]),
        pltpu.make_async_copy(pf_hbm, gates, sems.at[1]),
        pltpu.make_async_copy(pin_hbm, inputs, sems.at[2]),
        pltpu.make_async_copy(pk_hbm, pk, sems.at[3]),
        pltpu.make_async_copy(pv_hbm, pv, sems.at[4]),
    ]
    for copy in copies:
        copy.start()
    for copy in copies[:3]:
        copy.wait()
    ends = ends_of(len_ref)
    crowded = jnp.int32(0)
    for a, b in ((0, 1), (1, 2)):
        inside = (ends[a] // WIN == ends[b] // WIN) & (ends[a] % WIN != 0)
        crowded = jnp.where(inside, 1, crowded)
    flag[0] = crowded
    shape = (groups, LANES)
    pid = window_pid(me, ends)
    lane, row = iota(shape, 1), iota(shape, 0)

    def folded(ref):
        return jnp.concatenate(
            [ref[:, r * LANES : (r + 1) * LANES] for r in range(groups)], axis=0
        )

    lf = log_sigmoid(folded(gates))
    tail = lf
    step = 1
    while step < LANES:
        tail = tail + jnp.where(lane < LANES - step, pltpu.roll(tail, LANES - step, 1), 0.0)
        step *= 2
    after = jnp.broadcast_to(tail[:, 0:1], shape)
    after = jnp.where(row < groups - 1, pltpu.roll(after, groups - 1, 0), 0.0)
    step = 1
    while step < groups:
        after = after + jnp.where(row < groups - step, pltpu.roll(after, groups - step, 0), 0.0)
        step *= 2
    sums = [whole(jnp.where(pid == p, lf, 0.0)) for p in range(PROMPTS)]
    later = jnp.where(
        pid == 0,
        sums[1] + sums[2] + sums[3],
        jnp.where(pid == 1, sums[2] + sums[3], jnp.where(pid == 2, sums[3], 0.0)),
    )
    expo = folded(inputs) + ((tail - lf) + after - later)
    e_out[...] = expo
    weight = jnp.exp(expo)
    first = first_prompt(me, ends, slots)
    stacked = jnp.concatenate(
        [jnp.where(pid == first + s, weight, 0.0) for s in range(slots)]
        + [jnp.zeros((LANES - slots * groups, LANES), F32)],
        axis=0,
    )
    columns = stacked.T
    ashape = (AUX, LANES)
    arow, alane = iota(ashape, 0), iota(ashape, 1)
    aux = jnp.zeros(ashape, F32)
    for p in range(PROMPTS):
        rest = jnp.broadcast_to(sums[p], ashape)
        for part in range(3):
            piece = rest.astype(BF16).astype(F32)
            aux = jnp.where((arow == part) & (alane == p), piece, aux)
            rest = rest - piece
    aux = aux.astype(BF16)
    for dev in range(SEQ):
        msg[dev, slots * STATE : slots * STATE + AUX, :] = aux
    copies[3].wait()
    for r in range(groups):
        rows = slice(r * LANES, (r + 1) * LANES)
        keys = pk[rows, :].astype(F32)
        for s in range(slots):
            at = s * groups + r
            wmat[s, rows, :] = (keys * columns[:, at : at + 1]).astype(BF16)
    copies[4].wait()
    for s in range(slots):
        state = dot(wmat[s], pv[...], 0, 0).astype(BF16)
        for dev in range(SEQ):
            send_state(msg, dev, s, state[dev * ROWS : (dev + 1) * ROWS, :])


def spread_kernel(slots, len_ref, rp, m, expo, pk, unused, out, aft, acc, low, afters):
    me = lax.axis_index("seq")
    ends = ends_of(len_ref)
    shape = (SEQ, LANES)
    lane, row = iota(shape, 1), iota(shape, 0)
    base = slots * STATE
    gates = m[:, base : base + AUX, :].astype(F32)
    sums = gates[:, 2, :] + gates[:, 1, :] + gates[:, 0, :]
    after = jnp.where(row < SEQ - 1, pltpu.roll(sums, SEQ - 1, 0), 0.0)
    step = 1
    while step < SEQ:
        after = after + jnp.where(row < SEQ - step, pltpu.roll(after, SEQ - step, 0), 0.0)
        step *= 2
    afters[...] = after
    mine = jnp.broadcast_to(afters[pl.ds(me, 1), :], aft.shape)
    aft[...] = mine
    factor = jnp.exp(after)
    if slots == PROMPTS:
        first = jnp.zeros(shape, jnp.int32)
    else:
        first = prompt_at(row * WIN, ends)
    acc[...] = jnp.zeros_like(acc)
    for s in range(slots):
        scale = jnp.sum(jnp.where(lane == first + s, factor, 0.0), axis=1, keepdims=True)
        for dev in range(SEQ):
            p = first_prompt(dev, ends, slots) + s
            f = scale[dev : dev + 1, :]
            acc[p] += f * m[dev, s * STATE : (s + 1) * STATE, :].astype(F32)
    for p in range(PROMPTS):
        low[p] = acc[p].astype(BF16)
    groups = WIN // LANES
    pid = window_pid(me, ends)
    rest = jnp.zeros((groups, LANES), F32)
    for p in range(PROMPTS):
        rest = jnp.where(pid == p, mine[0:1, p : p + 1], rest)
    weight = jnp.exp(expo[...] + rest)
    columns = jnp.concatenate([weight, jnp.zeros((LANES - groups, LANES), F32)], axis=0).T
    mrow = iota((8, LANES), 0)
    norms = jnp.zeros((8, DK), F32)
    for r in range(groups):
        weighted = pk[r * LANES : (r + 1) * LANES, :].astype(F32) * columns[:, r : r + 1]
        member = (jnp.broadcast_to(pid[r : r + 1, :], (8, LANES)) == mrow).astype(F32)
        norms = norms + dot(member.astype(BF16), weighted.astype(BF16), 1, 0)
    aux = []
    for piece in split_two(norms):
        piece = piece.astype(F32)
        aux += [piece[0:PROMPTS, 0:LANES], piece[0:PROMPTS, LANES:DK]]
    aux = jnp.concatenate(aux, axis=0).astype(BF16)
    for dev in range(SEQ):
        for r in range(2):
            out[dev, r * STATE : (r + 1) * STATE, :] = low[rp[2 * dev + r, 0]]
        out[dev, 2 * STATE : 2 * STATE + NAUX, :] = aux


def respond_kernel(q, k, v, rin, rf, num, cols):
    shape = (8, RLEN)
    row, lane = iota(shape, 0), iota(shape, 1)
    gate = jnp.where(row == 0, rf[0, 0:1, :], rf[0, 1:2, :])
    cum = log_sigmoid(gate)
    step = 1
    while step < RLEN:
        cum = cum + jnp.where(lane >= step, pltpu.roll(cum, step, 1), 0.0)
        step *= 2
    tall = jnp.concatenate([cum, jnp.zeros((LANES - 8, RLEN), F32)], axis=0).T
    half = RLEN // 2
    clane = iota((RLEN, LANES), 1)
    packed = jnp.zeros((RLEN, LANES), F32)
    for r in range(2):
        ccol = tall[:, r : r + 1]
        srow = rin[0, r : r + 1, :] - cum[r : r + 1, :]
        for b in range(2):
            rows = slice(b * half, (b + 1) * half)
            width = (b + 1) * half
            scores = dot(q[r, rows, :], k[r, 0:width, :], 1, 1) * SCALE
            causal = iota((half, width), 0) + b * half >= iota((half, width), 1)
            decay = jnp.where(causal, ccol[rows, :] + srow[:, 0:width], -1e30)
            mixing = (scores * jnp.exp(decay)).astype(BF16)
            num[r, rows, :] = dot(mixing, v[r, 0:width, :], 1, 0).astype(BF16)
            den = jnp.sum(mixing.astype(F32), axis=1, keepdims=True)
            cols[rows, :] = jnp.where(
                clane[rows, :] == r, den, packed[rows, :] if r == 0 else cols[rows, :]
            )
        lifted = jnp.exp(ccol) * SCALE
        cols[...] = jnp.where(clane == 2 + r, lifted, cols[...])


def hidden_kernel(rp, q, m, num, cols, og, gain, hid, cols2, msg, nrm):
    me = lax.axis_index("seq")
    aux = jnp.sum(m[:, 2 * STATE : 2 * STATE + NAUX, :].astype(F32), axis=0)
    aux = aux[0:8, :] + aux[8:16, :]
    nrm[0:PROMPTS, :] = jnp.concatenate([aux[0:PROMPTS, :], aux[PROMPTS:8, :]], axis=1)
    clane = iota((GROUP, LANES), 1)
    sums = [jnp.zeros((GROUP, LANES), F32) for _ in range(RLEN // GROUP)]
    for r in range(2):
        norm = jnp.broadcast_to(nrm[pl.ds(rp[2 * me + r, 0], 1), :], (LANES, DK)).astype(BF16)
        state = received(m, r)
        for b in range(RLEN // GROUP):
            rows = slice(b * GROUP, (b + 1) * GROUP)
            small = cols[rows, :]
            lifted = small[:, 2 + r : 3 + r]
            query = q[r, rows, :]
            den = small[:, r : r + 1] + lifted * dot(query, norm, 1, 1)[:, 0:1]
            inverse = lax.rsqrt(den * den + 1.0)
            hidden = (num[r, rows, :].astype(F32) + lifted * dot(query, state, 1, 0)) * inverse
            hid[r, rows, :] = hidden.astype(BF16)
            squares = jnp.sum(hidden * hidden, axis=1, keepdims=True)
            dots = jnp.sum(og[r, rows, :].astype(F32) * gain[...] * hidden, axis=1, keepdims=True)
            lift = lifted * inverse
            total = sums[b]
            for at, value in (
                (2 * r, squares),
                (2 * r + 1, dots),
                (4 + r, lift),
                (6 + r, den * inverse * lift),
            ):
                total = jnp.where(clane == at, value, total)
            sums[b] = total
    rows8 = []
    for b in range(RLEN // GROUP):
        cols2[b * GROUP : (b + 1) * GROUP, :] = sums[b]
        turned = sums[b].T
        rows8 += [turned[0:4, c * LANES : (c + 1) * LANES] for c in range(GROUP // LANES)]
    rows = jnp.concatenate(rows8, axis=0)
    for dev in range(HEADS):
        msg[dev] = rows


def grad_kernel(m, hid, cols2, og, gain, q, msg, inv_out, numer, denom):
    total = m[0]
    for dev in range(1, HEADS):
        total = total + m[dev]
    features = HEADS * DV
    total = jnp.concatenate([total, jnp.zeros((LANES - 16, LANES), F32)], axis=0).T
    inverses = lax.rsqrt(total / features + 1e-6)
    coefs = pltpu.roll(total, LANES - 1, 1) * (inverses * inverses * inverses) / features
    inv_out[...] = inverses
    rows8 = []
    for r in range(2):
        for c in range(RLEN // LANES):
            rows = slice(c * LANES, (c + 1) * LANES)
            at = 4 * c + 2 * r
            inv, coef = inverses[:, at : at + 1], coefs[:, at : at + 1]
            small = cols2[rows, :]
            squares, dots = small[:, 2 * r : 2 * r + 1], small[:, 2 * r + 1 : 2 * r + 2]
            ratio = small[:, 6 + r : 7 + r]
            lift = small[:, 4 + r : 5 + r]
            grads = gain[...] * og[r, rows, :].astype(F32)
            numer[rows, :] = (grads * (inv * lift) - hid[r, rows, :].astype(F32) * (coef * lift)).astype(BF16)
            lift_denom = (-(inv * dots - coef * squares) * ratio).astype(BF16).astype(F32)
            part = jnp.sum(lift_denom * q[r, rows, :].astype(F32), axis=0, keepdims=True)
            denom[...] = part if c == 0 else denom[...] + part
        state = dot(q[r], numer[...], 0, 0).astype(BF16)
        for dev in range(SEQ):
            send_state(msg, dev, r, state[dev * ROWS : (dev + 1) * ROWS, :])
        for piece in split_two(denom[...]):
            piece = piece.astype(F32)
            rows8 += [piece[:, 0:LANES], piece[:, LANES:DK]]
    aux = jnp.concatenate(rows8, axis=0).astype(BF16)
    for dev in range(SEQ):
        msg[dev, 2 * STATE : 2 * STATE + AUX, :] = aux


def out_kernel(len_ref, hid, inverses, gain, expo, aft, pk, out, columns_out, weighted):
    me = lax.axis_index("seq")
    groups = WIN // LANES
    pid = window_pid(me, ends_of(len_ref))
    after = jnp.zeros((groups, LANES), F32)
    for p in range(PROMPTS):
        after = jnp.where(pid == p, aft[0:1, p : p + 1], after)
    weight = jnp.exp(expo[...] + after)
    columns = jnp.concatenate(
        [weight, pid.astype(F32), jnp.zeros((LANES - 2 * groups, LANES), F32)], axis=0
    ).T
    columns_out[...] = columns
    for r in range(groups):
        rows = slice(r * LANES, (r + 1) * LANES)
        weighted[rows, :] = (pk[rows, :].astype(F32) * columns[:, r : r + 1]).astype(BF16)
    for r in range(2):
        for c in range(RLEN // LANES):
            rows = slice(c * LANES, (c + 1) * LANES)
            at = 4 * c + 2 * r
            inv = inverses[:, at : at + 1]
            out[r, rows, :] = (hid[r, rows, :].astype(F32) * gain[...] * inv).astype(BF16)


def gather_kernel(slots, len_ref, rp, m, unused, out, gn, acc, aacc, low):
    ends = ends_of(len_ref)
    acc[...] = jnp.zeros_like(acc)
    aacc[...] = jnp.zeros_like(aacc)
    for dev in range(SEQ):
        for r in range(2):
            p = rp[2 * dev + r, 0]
            acc[p] += m[dev, r * STATE : (r + 1) * STATE, :].astype(F32)
            aacc[r, p] += m[dev, 2 * STATE : 2 * STATE + AUX, :].astype(F32)
    for p in range(PROMPTS):
        low[p] = acc[p].astype(BF16)
        total = jnp.zeros((2, LANES), F32)
        for r in range(2):
            total = total + (aacc[r, p, 4 * r : 4 * r + 2, :] + aacc[r, p, 4 * r + 2 : 4 * r + 4, :])
        total = total.astype(BF16).astype(F32)
        gn[p : p + 1, :] = jnp.concatenate([total[0:1, :], total[1:2, :]], axis=1)
    gn[PROMPTS:, :] = jnp.zeros((8 - PROMPTS, DK), F32)
    for dev in range(SEQ):
        first = first_prompt(dev, ends, slots)
        for s in range(slots):
            out[dev, s * STATE : (s + 1) * STATE, :] = low[jnp.minimum(first + s, PROMPTS - 1)]


def prompt_kernel(
    slots, len_ref, m, gn, columns_ref, weighted_ref, pv, kg_hbm, vg_hbm, kg, vg, sems
):
    me = lax.axis_index("seq")
    ends = ends_of(len_ref)
    groups = WIN // LANES
    first = first_prompt(me, ends, slots)
    columns = columns_ref[...]

    def at_row(j):
        total = jnp.int32(0)
        for e in ends:
            total = total + jnp.where(me * WIN + j >= e, 1, 0)
        return total

    copies = []
    per = GROUP // LANES
    for g in range(WIN // GROUP):
        rows = slice(g * GROUP, (g + 1) * GROUP)
        w, ids = (
            jnp.concatenate(
                [columns[:, at + g * per + i : at + g * per + i + 1] for i in range(per)], axis=0
            )
            for at in (0, groups)
        )
        weighted = weighted_ref[rows, :]
        low, high = at_row(g * GROUP), at_row((g + 1) * GROUP - 1)

        def grads(p):
            grad = received(m, p - first)
            value_grad = dot(weighted, grad, 1, 0)
            key_grad = w * (dot(pv[rows, :], grad, 1, 1) + gn[pl.ds(p, 1), :])
            return key_grad.astype(BF16), value_grad.astype(BF16)

        kg[rows, :], vg[rows, :] = grads(low)

        @pl.loop(low + 1, high + 1)
        def _(p):
            key_grad, value_grad = grads(p)
            mine = ids == p.astype(F32)
            kg[rows, :] = jnp.where(mine, key_grad, kg[rows, :])
            vg[rows, :] = jnp.where(mine, value_grad, vg[rows, :])

        copies += [
            pltpu.make_async_copy(kg.at[rows], kg_hbm.at[rows], sems.at[2 * g]),
            pltpu.make_async_copy(vg.at[rows], vg_hbm.at[rows], sems.at[2 * g + 1]),
        ]
        for copy in copies[-2:]:
            copy.start()
    for copy in copies:
        copy.wait()


def exchange(x, axis):
    return lax.all_to_all(x, axis, 0, 0, tiled=True)


def states(slots, pk, pv, pin, pf, lengths):
    groups = WIN // LANES
    return call(
        functools.partial(state_kernel, slots),
        [HBM] * 5,
        [
            ((SEQ, slots * STATE + AUX, LANES), BF16),
            ((groups, LANES), F32),
            ((1,), jnp.int32),
        ],
        [
            pltpu.SMEM((PROMPTS,), jnp.int32),
            pltpu.VMEM((1, WIN), F32),
            pltpu.VMEM((1, WIN), F32),
            pltpu.VMEM((WIN, DK), BF16),
            pltpu.VMEM((WIN, DV), BF16),
            pltpu.VMEM((slots, WIN, DK), BF16),
            pltpu.SemaphoreType.DMA((5,)),
        ],
        spec=(VMEM, VMEM, SMEM),
        name="state_kernel",
    )(lengths, pk, pv, pin, pf)


def rest(slots, got1, expo, num, cols, pk, pv, pin, pf, lengths, rp, q, gain, og):
    part = functools.partial
    if slots > 2:
        msg1, expo, _ = states(slots, pk, pv, pin, pf, lengths)
        got1 = exchange(msg1, "seq")
    msg2, aft = call(
        part(spread_kernel, slots),
        [SMEM, SMEM] + [VMEM] * 3 + [ANY],
        [((SEQ, 2 * STATE + NAUX, LANES), BF16), ((8, LANES), F32)],
        [
            pltpu.VMEM((PROMPTS + slots, STATE, LANES), F32),
            pltpu.VMEM((PROMPTS, STATE, LANES), BF16),
            pltpu.VMEM((SEQ, LANES), F32),
        ],
        name="spread_kernel",
    )(lengths, rp, got1, expo, pk, cols)
    got2 = exchange(msg2, "seq")
    hid, cols2, msg3 = call(
        hidden_kernel,
        [SMEM] + [VMEM] * 6,
        [((2, RLEN, DV), BF16), ((RLEN, LANES), F32), ((HEADS, 16, LANES), F32)],
        [pltpu.VMEM((8, DK), F32)],
        name="hidden_kernel",
    )(rp, q, got2, num, cols, og, gain)
    got3 = exchange(msg3, "head")
    msg4, inverses = call(
        grad_kernel,
        [VMEM] * 6,
        [((SEQ, 2 * STATE + AUX, LANES), BF16), ((LANES, LANES), F32)],
        [pltpu.VMEM((RLEN, DV), BF16), pltpu.VMEM((1, DK), F32)],
        name="grad_kernel",
    )(got3, hid, cols2, og, gain, q)
    got4 = exchange(msg4, "seq")
    resp_out, columns, weighted = call(
        out_kernel,
        [SMEM] + [VMEM] * 6,
        [((2, RLEN, DV), BF16), ((LANES, LANES), F32), ((WIN, DK), BF16)],
        [],
        name="out_kernel",
    )(lengths, hid, inverses, gain, expo, aft, pk)
    msg5, gn = call(
        part(gather_kernel, slots),
        [SMEM, SMEM, VMEM, ANY],
        [((SEQ, slots * STATE, LANES), BF16), ((8, DK), F32)],
        [
            pltpu.VMEM((PROMPTS, STATE, LANES), F32),
            pltpu.VMEM((2, PROMPTS, AUX, LANES), F32),
            pltpu.VMEM((PROMPTS, STATE, LANES), BF16),
        ],
        name="gather_kernel",
    )(lengths, rp, got4, columns)
    got5 = exchange(msg5, "seq")
    key_grad, value_grad = call(
        part(prompt_kernel, slots),
        [SMEM] + [VMEM] * 5,
        [((WIN, DK), BF16), ((WIN, DV), BF16)],
        [
            pltpu.VMEM((WIN, DK), BF16),
            pltpu.VMEM((WIN, DV), BF16),
            pltpu.SemaphoreType.DMA((2 * WIN // GROUP,)),
        ],
        spec=HBM,
        name="prompt_kernel",
    )(lengths, got5, gn, columns, weighted, pv)
    return resp_out, key_grad, value_grad


def local(pk, pv, pin, pf, lengths, rp, q, k, v, rin, rf, gain, og):
    msg1, expo, flag = states(2, pk, pv, pin, pf, lengths)
    got1 = exchange(msg1, "seq")
    num, cols = call(
        respond_kernel,
        [VMEM] * 5,
        [((2, RLEN, DV), BF16), ((RLEN, LANES), F32)],
        [],
        name="respond_kernel",
    )(q, k, v, rin, rf)
    args = (got1, expo, num, cols, pk, pv, pin, pf, lengths, rp, q, gain.reshape(1, DV), og)
    return lax.cond(
        flag[0] > 0, functools.partial(rest, PROMPTS), functools.partial(rest, 2), *args
    )


def solution(mesh):
    in_specs = (
        P("seq", "head"),
        P("seq", "head"),
        P("head", "seq"),
        P("head", "seq"),
        P(),
        P(),
        P("seq", None, "head"),
        P("seq", None, "head"),
        P("seq", None, "head"),
        P("head", "seq", None),
        P("head", "seq", None),
        P("head"),
        P("seq", None, "head"),
    )
    out_specs = (P("seq", None, "head"), P("seq", "head"), P("seq", "head"))
    return jax.shard_map(local, mesh=mesh, in_specs=in_specs, out_specs=out_specs, check_vma=False)
```

```python
import functools

import jax
import jax.numpy as jnp
from jax import lax
from jax.experimental import pallas as pl
from jax.experimental.pallas import tpu as pltpu
from jax.sharding import PartitionSpec as P

F32 = jnp.float32
BF16 = jnp.bfloat16
PROMPTS = 4
SEQ = 16
HEADS = 8
DK = 256
DV = 512
WIN = 1024
RLEN = 512
ROWS = DK // SEQ
LANES = 128
TILES = DV // LANES
STATE = ROWS * TILES
AUX = 8
NAUX = 16
GROUP = 256
SCALE = DK ** (-0.5)

VMEM = pl.BlockSpec(memory_space=pltpu.VMEM)
SMEM = pl.BlockSpec(memory_space=pltpu.SMEM)
HBM = pl.BlockSpec(memory_space=pltpu.HBM)
ANY = pl.BlockSpec(memory_space=pl.ANY)


def call(body, ins, outs, scratch, spec=VMEM, **kw):
    return pl.pallas_call(
        body,
        in_specs=ins,
        out_specs=spec if isinstance(spec, tuple) else tuple(spec for _ in outs),
        out_shape=tuple(jax.ShapeDtypeStruct(s, d) for s, d in outs),
        scratch_shapes=scratch,
        compiler_params=pltpu.CompilerParams(vmem_limit_bytes=24 << 20),
        **kw,
    )


def iota(shape, dim):
    return lax.broadcasted_iota(jnp.int32, shape, dim)


def ends_of(len_ref):
    e0 = len_ref[0]
    e1 = e0 + len_ref[1]
    e2 = e1 + len_ref[2]
    return e0, e1, e2


def prompt_at(position, ends):
    total = 0
    for e in ends:
        total = total + (position >= e).astype(jnp.int32)
    return total


def first_prompt(device, ends, slots):
    if slots == PROMPTS:
        return 0
    total = jnp.int32(0)
    for e in ends:
        total = total + jnp.where(device * WIN >= e, 1, 0)
    return total


def log_sigmoid(x):
    return jnp.minimum(x, 0.0) - jnp.log1p(jnp.exp(-jnp.abs(x)))


def dot(a, b, ca, cb):
    return lax.dot_general(a, b, (((ca,), (cb,)), ((), ())), preferred_element_type=F32)


def split_two(x):
    hi = x.astype(BF16)
    return hi, (x - hi.astype(F32)).astype(BF16)


def send_state(msg, dev, slot, rows):
    for c in range(TILES):
        at = slot * STATE + c * ROWS
        msg[dev, at : at + ROWS, :] = rows[:, c * LANES : (c + 1) * LANES]


def received(m, slot):
    tiles = []
    for c in range(TILES):
        start = slot * STATE + c * ROWS
        if not isinstance(start, int):
            start = pl.multiple_of(start, ROWS)
        tiles.append(m[:, pl.ds(start, ROWS), :].reshape(DK, LANES))
    return jnp.concatenate(tiles, axis=1)


def whole(x):
    return jnp.sum(jnp.sum(x, axis=0, keepdims=True), axis=1, keepdims=True)


def window_pid(me, ends):
    shape = (WIN // LANES, LANES)
    return prompt_at(me * WIN + iota(shape, 0) * LANES + iota(shape, 1), ends)


def state_kernel(
    slots, len_hbm, pk_hbm, pv_hbm, pin_hbm, pf_hbm, msg, e_out, flag, len_ref, gates, inputs, pk, pv, wmat, sems
):
    me = lax.axis_index("seq")
    groups = WIN // LANES
    copies = [
        pltpu.make_async_copy(len_hbm, len_ref, sems.at[0]),
        pltpu.make_async_copy(pf_hbm, gates, sems.at[1]),
        pltpu.make_async_copy(pin_hbm, inputs, sems.at[2]),
        pltpu.make_async_copy(pk_hbm, pk, sems.at[3]),
        pltpu.make_async_copy(pv_hbm, pv, sems.at[4]),
    ]
    for copy in copies:
        copy.start()
    for copy in copies[:3]:
        copy.wait()
    ends = ends_of(len_ref)
    crowded = jnp.int32(0)
    for a, b in ((0, 1), (1, 2)):
        inside = (ends[a] // WIN == ends[b] // WIN) & (ends[a] % WIN != 0)
        crowded = jnp.where(inside, 1, crowded)
    flag[0] = crowded
    shape = (groups, LANES)
    pid = window_pid(me, ends)
    lane, row = iota(shape, 1), iota(shape, 0)

    def folded(ref):
        return jnp.concatenate(
            [ref[:, r * LANES : (r + 1) * LANES] for r in range(groups)], axis=0
        )

    lf = log_sigmoid(folded(gates))
    tail = lf
    step = 1
    while step < LANES:
        tail = tail + jnp.where(lane < LANES - step, pltpu.roll(tail, LANES - step, 1), 0.0)
        step *= 2
    after = jnp.broadcast_to(tail[:, 0:1], shape)
    after = jnp.where(row < groups - 1, pltpu.roll(after, groups - 1, 0), 0.0)
    step = 1
    while step < groups:
        after = after + jnp.where(row < groups - step, pltpu.roll(after, groups - step, 0), 0.0)
        step *= 2
    sums = [whole(jnp.where(pid == p, lf, 0.0)) for p in range(PROMPTS)]
    later = jnp.where(
        pid == 0,
        sums[1] + sums[2] + sums[3],
        jnp.where(pid == 1, sums[2] + sums[3], jnp.where(pid == 2, sums[3], 0.0)),
    )
    expo = folded(inputs) + ((tail - lf) + after - later)
    e_out[...] = expo
    weight = jnp.exp(expo)
    first = first_prompt(me, ends, slots)
    stacked = jnp.concatenate(
        [jnp.where(pid == first + s, weight, 0.0) for s in range(slots)]
        + [jnp.zeros((LANES - slots * groups, LANES), F32)],
        axis=0,
    )
    columns = stacked.T
    ashape = (AUX, LANES)
    arow, alane = iota(ashape, 0), iota(ashape, 1)
    aux = jnp.zeros(ashape, F32)
    for p in range(PROMPTS):
        rest = jnp.broadcast_to(sums[p], ashape)
        for part in range(3):
            piece = rest.astype(BF16).astype(F32)
            aux = jnp.where((arow == part) & (alane == p), piece, aux)
            rest = rest - piece
    aux = aux.astype(BF16)
    for dev in range(SEQ):
        msg[dev, slots * STATE : slots * STATE + AUX, :] = aux
    copies[3].wait()
    for r in range(groups):
        rows = slice(r * LANES, (r + 1) * LANES)
        keys = pk[rows, :].astype(F32)
        for s in range(slots):
            at = s * groups + r
            wmat[s, rows, :] = (keys * columns[:, at : at + 1]).astype(BF16)
    copies[4].wait()
    for s in range(slots):
        state = dot(wmat[s], pv[...], 0, 0).astype(BF16)
        for dev in range(SEQ):
            send_state(msg, dev, s, state[dev * ROWS : (dev + 1) * ROWS, :])


def spread_kernel(slots, len_ref, rp, m, expo, pk, unused, out, aft, acc, low, afters):
    me = lax.axis_index("seq")
    ends = ends_of(len_ref)
    shape = (SEQ, LANES)
    lane, row = iota(shape, 1), iota(shape, 0)
    base = slots * STATE
    gates = m[:, base : base + AUX, :].astype(F32)
    sums = gates[:, 2, :] + gates[:, 1, :] + gates[:, 0, :]
    after = jnp.where(row < SEQ - 1, pltpu.roll(sums, SEQ - 1, 0), 0.0)
    step = 1
    while step < SEQ:
        after = after + jnp.where(row < SEQ - step, pltpu.roll(after, SEQ - step, 0), 0.0)
        step *= 2
    afters[...] = after
    mine = jnp.broadcast_to(afters[pl.ds(me, 1), :], aft.shape)
    aft[...] = mine
    factor = jnp.exp(after)
    if slots == PROMPTS:
        first = jnp.zeros(shape, jnp.int32)
    else:
        first = prompt_at(row * WIN, ends)
    acc[...] = jnp.zeros_like(acc)
    for s in range(slots):
        scale = jnp.sum(jnp.where(lane == first + s, factor, 0.0), axis=1, keepdims=True)
        for dev in range(SEQ):
            p = first_prompt(dev, ends, slots) + s
            f = scale[dev : dev + 1, :]
            acc[p] += f * m[dev, s * STATE : (s + 1) * STATE, :].astype(F32)
    for p in range(PROMPTS):
        low[p] = acc[p].astype(BF16)
    groups = WIN // LANES
    pid = window_pid(me, ends)
    rest = jnp.zeros((groups, LANES), F32)
    for p in range(PROMPTS):
        rest = jnp.where(pid == p, mine[0:1, p : p + 1], rest)
    weight = jnp.exp(expo[...] + rest)
    columns = jnp.concatenate([weight, jnp.zeros((LANES - groups, LANES), F32)], axis=0).T
    mrow = iota((8, LANES), 0)
    norms = jnp.zeros((8, DK), F32)
    for r in range(groups):
        weighted = pk[r * LANES : (r + 1) * LANES, :].astype(F32) * columns[:, r : r + 1]
        member = (jnp.broadcast_to(pid[r : r + 1, :], (8, LANES)) == mrow).astype(F32)
        norms = norms + dot(member.astype(BF16), weighted.astype(BF16), 1, 0)
    aux = []
    for piece in split_two(norms):
        piece = piece.astype(F32)
        aux += [piece[0:PROMPTS, 0:LANES], piece[0:PROMPTS, LANES:DK]]
    aux = jnp.concatenate(aux, axis=0).astype(BF16)
    for dev in range(SEQ):
        for r in range(2):
            out[dev, r * STATE : (r + 1) * STATE, :] = low[rp[2 * dev + r, 0]]
        out[dev, 2 * STATE : 2 * STATE + NAUX, :] = aux


def respond_kernel(q, k, v, rin, rf, num, cols):
    shape = (8, RLEN)
    row, lane = iota(shape, 0), iota(shape, 1)
    gate = jnp.where(row == 0, rf[0, 0:1, :], rf[0, 1:2, :])
    cum = log_sigmoid(gate)
    step = 1
    while step < RLEN:
        cum = cum + jnp.where(lane >= step, pltpu.roll(cum, step, 1), 0.0)
        step *= 2
    tall = jnp.concatenate([cum, jnp.zeros((LANES - 8, RLEN), F32)], axis=0).T
    half = RLEN // 2
    clane = iota((RLEN, LANES), 1)
    packed = jnp.zeros((RLEN, LANES), F32)
    for r in range(2):
        ccol = tall[:, r : r + 1]
        srow = rin[0, r : r + 1, :] - cum[r : r + 1, :]
        for b in range(2):
            rows = slice(b * half, (b + 1) * half)
            width = (b + 1) * half
            scores = dot(q[r, rows, :], k[r, 0:width, :], 1, 1) * SCALE
            causal = iota((half, width), 0) + b * half >= iota((half, width), 1)
            decay = jnp.where(causal, ccol[rows, :] + srow[:, 0:width], -1e30)
            mixing = (scores * jnp.exp(decay)).astype(BF16)
            num[r, rows, :] = dot(mixing, v[r, 0:width, :], 1, 0).astype(BF16)
            den = jnp.sum(mixing.astype(F32), axis=1, keepdims=True)
            cols[rows, :] = jnp.where(
                clane[rows, :] == r, den, packed[rows, :] if r == 0 else cols[rows, :]
            )
        lifted = jnp.exp(ccol) * SCALE
        cols[...] = jnp.where(clane == 2 + r, lifted, cols[...])


def hidden_kernel(rp, q, m, num, cols, og, gain, hid, cols2, msg, nrm):
    me = lax.axis_index("seq")
    aux = jnp.sum(m[:, 2 * STATE : 2 * STATE + NAUX, :].astype(F32), axis=0)
    aux = aux[0:8, :] + aux[8:16, :]
    nrm[0:PROMPTS, :] = jnp.concatenate([aux[0:PROMPTS, :], aux[PROMPTS:8, :]], axis=1)
    clane = iota((GROUP, LANES), 1)
    ones = jnp.ones((2 * LANES, LANES), BF16)
    sums = [jnp.zeros((GROUP, LANES), F32) for _ in range(RLEN // GROUP)]

    def row_sum(x):
        return dot(jnp.concatenate(split_two(x), axis=1), ones, 1, 0)

    for r in range(2):
        norm = jnp.broadcast_to(nrm[pl.ds(rp[2 * me + r, 0], 1), :], (LANES, DK)).astype(BF16)
        state = received(m, r)
        for b in range(RLEN // GROUP):
            rows = slice(b * GROUP, (b + 1) * GROUP)
            lifted = jnp.broadcast_to(cols[rows, 2 + r : 3 + r], (GROUP, LANES))
            den = jnp.broadcast_to(cols[rows, r : r + 1], (GROUP, LANES))
            query = q[r, rows, :]
            den = den + lifted * dot(query, norm, 1, 1)
            inverse = lax.rsqrt(den * den + 1.0)
            lift = lifted * inverse
            squares = jnp.zeros((GROUP, LANES), F32)
            dots = jnp.zeros((GROUP, LANES), F32)
            for c in range(TILES):
                tile = slice(c * LANES, (c + 1) * LANES)
                if c % 2 == 0:
                    pair = slice(c * LANES, (c + 2) * LANES)
                    both = dot(query, state[:, pair], 1, 0)
                lifting = both[:, (c % 2) * LANES : (c % 2 + 1) * LANES]
                hidden = (num[r, rows, tile].astype(F32) + lifted * lifting) * inverse
                hid[r, rows, tile] = hidden.astype(BF16)
                squares = squares + hidden * hidden
                dots = dots + og[r, rows, tile].astype(F32) * gain[:, tile] * hidden
            total = sums[b]
            for at, value in (
                (2 * r, row_sum(squares)),
                (2 * r + 1, row_sum(dots)),
                (16 + 2 * r, lift),
                (32 + 2 * r, den * inverse * lift),
            ):
                total = jnp.where(clane == at, value, total)
            sums[b] = total
    rows8 = []
    for b in range(RLEN // GROUP):
        cols2[b * GROUP : (b + 1) * GROUP, :] = sums[b]
        turned = sums[b].T
        rows8 += [turned[0:4, c * LANES : (c + 1) * LANES] for c in range(GROUP // LANES)]
    rows = jnp.concatenate(rows8, axis=0)
    for dev in range(HEADS):
        msg[dev] = rows


def grad_kernel(m, hid, cols2, og, gain, q, msg, out_hbm, numer, denom, out, sems):
    total = m[0]
    for dev in range(1, HEADS):
        total = total + m[dev]
    features = HEADS * DV
    total = jnp.concatenate([total, jnp.zeros((LANES - 16, LANES), F32)], axis=0).T
    inverses = lax.rsqrt(total / features + 1e-6)
    coefs = pltpu.roll(total, LANES - 1, 1) * (inverses * inverses * inverses) / features
    copies = []
    for c in range(RLEN // LANES):
        rows = slice(c * LANES, (c + 1) * LANES)
        shift = (LANES - 4 * c) % LANES
        inv = pltpu.roll(inverses, shift, 1) if shift else inverses
        coef = pltpu.roll(coefs, shift, 1) if shift else coefs
        squares = cols2[rows, :]
        dots = pltpu.roll(squares, LANES - 1, 1)
        lift = pltpu.roll(squares, LANES - 16, 1)
        ratio = pltpu.roll(squares, LANES - 32, 1)
        small = -(inv * dots - coef * squares) * ratio
        lane = iota((LANES, LANES), 1)
        useful = (lane == 0) | (lane == 2)
        denom[rows, :] = jnp.where(useful, small, 0.0).astype(BF16)
        by_grad, by_hidden = inv * lift, coef * lift
        for r in range(2):
            at = slice(2 * r, 2 * r + 1)
            grads = gain[...] * og[r, rows, :].astype(F32)
            hidden = hid[r, rows, :].astype(F32)
            numer[r, rows, :] = (grads * by_grad[:, at] - hidden * by_hidden[:, at]).astype(BF16)
            out[r, rows, :] = (hidden * gain[...] * inv[:, at]).astype(BF16)
            place = pl.ds(c * LANES, LANES)
            copies.append(
                pltpu.make_async_copy(out.at[r, place], out_hbm.at[r, place], sems.at[2 * c + r])
            )
            copies[-1].start()
    rows8 = []
    for r in range(2):
        state = dot(q[r], numer[r], 0, 0).astype(BF16)
        for dev in range(SEQ):
            send_state(msg, dev, r, state[dev * ROWS : (dev + 1) * ROWS, :])
        norm = dot(denom[...], q[r], 0, 0)[2 * r : 2 * r + 1, :]
        for piece in split_two(norm):
            piece = piece.astype(F32)
            rows8 += [piece[:, 0:LANES], piece[:, LANES:DK]]
    aux = jnp.concatenate(rows8, axis=0).astype(BF16)
    for dev in range(SEQ):
        msg[dev, 2 * STATE : 2 * STATE + AUX, :] = aux
    for copy in copies:
        copy.wait()


def gather_kernel(slots, len_ref, rp, m, out, gn, acc, aacc, low):
    ends = ends_of(len_ref)
    acc[...] = jnp.zeros_like(acc)
    aacc[...] = jnp.zeros_like(aacc)
    for dev in range(SEQ):
        for r in range(2):
            p = rp[2 * dev + r, 0]
            acc[p] += m[dev, r * STATE : (r + 1) * STATE, :].astype(F32)
            aacc[r, p] += m[dev, 2 * STATE : 2 * STATE + AUX, :].astype(F32)
    for p in range(PROMPTS):
        low[p] = acc[p].astype(BF16)
        total = jnp.zeros((2, LANES), F32)
        for r in range(2):
            total = total + (aacc[r, p, 4 * r : 4 * r + 2, :] + aacc[r, p, 4 * r + 2 : 4 * r + 4, :])
        total = total.astype(BF16).astype(F32)
        gn[p : p + 1, :] = jnp.concatenate([total[0:1, :], total[1:2, :]], axis=1)
    gn[PROMPTS:, :] = jnp.zeros((8 - PROMPTS, DK), F32)
    for dev in range(SEQ):
        first = first_prompt(dev, ends, slots)
        for s in range(slots):
            out[dev, s * STATE : (s + 1) * STATE, :] = low[jnp.minimum(first + s, PROMPTS - 1)]


def prompt_kernel(
    slots, len_ref, m, gn, expo, aft, pk, pv, kg_hbm, vg_hbm, kg, vg, sems
):
    me = lax.axis_index("seq")
    ends = ends_of(len_ref)
    groups = WIN // LANES
    first = first_prompt(me, ends, slots)
    pid = window_pid(me, ends)
    after = jnp.zeros((groups, LANES), F32)
    for p in range(PROMPTS):
        after = jnp.where(pid == p, aft[0:1, p : p + 1], after)
    weight = jnp.exp(expo[...] + after)
    columns = jnp.concatenate(
        [weight, pid.astype(F32), jnp.zeros((LANES - 2 * groups, LANES), F32)], axis=0
    ).T

    def at_row(j):
        total = jnp.int32(0)
        for e in ends:
            total = total + jnp.where(me * WIN + j >= e, 1, 0)
        return total

    copies = []
    per = GROUP // LANES
    for g in range(WIN // GROUP):
        rows = slice(g * GROUP, (g + 1) * GROUP)
        w, ids = (
            jnp.concatenate(
                [columns[:, at + g * per + i : at + g * per + i + 1] for i in range(per)], axis=0
            )
            for at in (0, groups)
        )
        weighted = (pk[rows, :].astype(F32) * w).astype(BF16)
        low, high = at_row(g * GROUP), at_row((g + 1) * GROUP - 1)

        def grads(p):
            grad = received(m, p - first)
            value_grad = dot(weighted, grad, 1, 0)
            key_grad = w * (dot(pv[rows, :], grad, 1, 1) + gn[pl.ds(p, 1), :])
            return key_grad.astype(BF16), value_grad.astype(BF16)

        kg[rows, :], vg[rows, :] = grads(low)

        @pl.loop(low + 1, high + 1)
        def _(p):
            key_grad, value_grad = grads(p)
            mine = ids == p.astype(F32)
            kg[rows, :] = jnp.where(mine, key_grad, kg[rows, :])
            vg[rows, :] = jnp.where(mine, value_grad, vg[rows, :])

        copies += [
            pltpu.make_async_copy(kg.at[rows], kg_hbm.at[rows], sems.at[2 * g]),
            pltpu.make_async_copy(vg.at[rows], vg_hbm.at[rows], sems.at[2 * g + 1]),
        ]
        for copy in copies[-2:]:
            copy.start()
    for copy in copies:
        copy.wait()


def exchange(x, axis):
    return lax.all_to_all(x, axis, 0, 0, tiled=True)


def states(slots, pk, pv, pin, pf, lengths):
    groups = WIN // LANES
    return call(
        functools.partial(state_kernel, slots),
        [HBM] * 5,
        [
            ((SEQ, slots * STATE + AUX, LANES), BF16),
            ((groups, LANES), F32),
            ((1,), jnp.int32),
        ],
        [
            pltpu.SMEM((PROMPTS,), jnp.int32),
            pltpu.VMEM((1, WIN), F32),
            pltpu.VMEM((1, WIN), F32),
            pltpu.VMEM((WIN, DK), BF16),
            pltpu.VMEM((WIN, DV), BF16),
            pltpu.VMEM((slots, WIN, DK), BF16),
            pltpu.SemaphoreType.DMA((5,)),
        ],
        spec=(VMEM, VMEM, SMEM),
        name="state_kernel",
    )(lengths, pk, pv, pin, pf)


def rest(slots, got1, expo, num, cols, pk, pv, pin, pf, lengths, rp, q, gain, og):
    part = functools.partial
    if slots > 2:
        msg1, expo, _ = states(slots, pk, pv, pin, pf, lengths)
        got1 = exchange(msg1, "seq")
    msg2, aft = call(
        part(spread_kernel, slots),
        [SMEM, SMEM] + [VMEM] * 3 + [ANY],
        [((SEQ, 2 * STATE + NAUX, LANES), BF16), ((8, LANES), F32)],
        [
            pltpu.VMEM((PROMPTS + slots, STATE, LANES), F32),
            pltpu.VMEM((PROMPTS, STATE, LANES), BF16),
            pltpu.VMEM((SEQ, LANES), F32),
        ],
        name="spread_kernel",
    )(lengths, rp, got1, expo, pk, cols)
    got2 = exchange(msg2, "seq")
    hid, cols2, msg3 = call(
        hidden_kernel,
        [SMEM] + [VMEM] * 6,
        [((2, RLEN, DV), BF16), ((RLEN, LANES), F32), ((HEADS, 16, LANES), F32)],
        [pltpu.VMEM((8, DK), F32)],
        name="hidden_kernel",
    )(rp, q, got2, num, cols, og, gain)
    got3 = exchange(msg3, "head")
    msg4, resp_out = call(
        grad_kernel,
        [VMEM] * 6,
        [((SEQ, 2 * STATE + AUX, LANES), BF16), ((2, RLEN, DV), BF16)],
        [
            pltpu.VMEM((2, RLEN, DV), BF16),
            pltpu.VMEM((RLEN, LANES), BF16),
            pltpu.VMEM((2, RLEN, DV), BF16),
            pltpu.SemaphoreType.DMA((2 * RLEN // LANES,)),
        ],
        spec=(VMEM, HBM),
        name="grad_kernel",
    )(got3, hid, cols2, og, gain, q)
    got4 = exchange(msg4, "seq")
    msg5, gn = call(
        part(gather_kernel, slots),
        [SMEM, SMEM, VMEM],
        [((SEQ, slots * STATE, LANES), BF16), ((8, DK), F32)],
        [
            pltpu.VMEM((PROMPTS, STATE, LANES), F32),
            pltpu.VMEM((2, PROMPTS, AUX, LANES), F32),
            pltpu.VMEM((PROMPTS, STATE, LANES), BF16),
        ],
        name="gather_kernel",
    )(lengths, rp, got4)
    got5 = exchange(msg5, "seq")
    key_grad, value_grad = call(
        part(prompt_kernel, slots),
        [SMEM] + [VMEM] * 6,
        [((WIN, DK), BF16), ((WIN, DV), BF16)],
        [
            pltpu.VMEM((WIN, DK), BF16),
            pltpu.VMEM((WIN, DV), BF16),
            pltpu.SemaphoreType.DMA((2 * WIN // GROUP,)),
        ],
        spec=HBM,
        name="prompt_kernel",
    )(lengths, got5, gn, expo, aft, pk, pv)
    return resp_out, key_grad, value_grad


def local(pk, pv, pin, pf, lengths, rp, q, k, v, rin, rf, gain, og):
    msg1, expo, flag = states(2, pk, pv, pin, pf, lengths)
    got1 = exchange(msg1, "seq")
    num, cols = call(
        respond_kernel,
        [VMEM] * 5,
        [((2, RLEN, DV), BF16), ((RLEN, LANES), F32)],
        [],
        name="respond_kernel",
    )(q, k, v, rin, rf)
    args = (got1, expo, num, cols, pk, pv, pin, pf, lengths, rp, q, gain.reshape(1, DV), og)
    return lax.cond(
        flag[0] > 0, functools.partial(rest, PROMPTS), functools.partial(rest, 2), *args
    )


def solution(mesh):
    in_specs = (
        P("seq", "head"),
        P("seq", "head"),
        P("head", "seq"),
        P("head", "seq"),
        P(),
        P(),
        P("seq", None, "head"),
        P("seq", None, "head"),
        P("seq", None, "head"),
        P("head", "seq", None),
        P("head", "seq", None),
        P("head"),
        P("seq", None, "head"),
    )
    out_specs = (P("seq", None, "head"), P("seq", "head"), P("seq", "head"))
    return jax.shard_map(local, mesh=mesh, in_specs=in_specs, out_specs=out_specs, check_vma=False)
```
